32 devices in a mesh: az: 8 (over y, x, core), ax: 4 (over z).
Axes of the slice: x: 2, y: 2, z: 4, core: 2. Of those that a mesh axis runs over, the one named last changes fastest.
Arguments:
- step_start: float32 [5, 16, 512, 2048], P(None, None, 'ax', 'az'), may hold values from -3 to 12, as said below
- section_state: float32 [5, 16, 512, 2048], P(None, None, 'ax', 'az'), may hold values from -3 to 12, as said below
- near_rows: int32 [512], P('ax'), may hold values from 1 to 4
- cutoff: int32 [4, 512], P(None, 'ax'), may hold values from 64 to 511
- gore_map: int32 [512, 2048], P('ax', 'az'), may hold values from 0 to 80, as said below
Outputs:
- new_state: float32 [5, 16, 512, 2048], P(None, None, 'ax', 'az')
- gore_loads: float32 [80], replicated
The draws below stay inside these ranges and needn't reach their ends.
Inputs may be any that keep to these rules, and one draw needn't show every extreme that they name: `step_start`: every cell holds density, momentum and total energy of a gas state whose density and pressure lie between 0.5 and 2 and whose velocity components lie within 1.5 in magnitude. `section_state`: every cell holds density, momentum and total energy of a gas state whose density and pressure lie between 0.5 and 2 and whose velocity components lie within 1.5 in magnitude. `gore_map`: each axial station is either entirely gap, marked 80, or canopy whose gores run in azimuthal bands.
All inputs are finite; a program needn't handle non-finite values.
Results may differ from the reference program's by a relative error of at most 0.000077.
Values sent between devices are 32-bit elements; how exact they have to be, the bound alone decides.
A program may use at most 192 MiB of HBM per device.

```python
import math
import jax
import jax.numpy as jnp
from jax import lax

NA = 2048
NR = 16
NF = 4
GORES = 80
NX = 512


def flow_state(key):
    key_density, key_speed, key_pressure = jax.random.split(key, 3)
    grid_shape = (NR, NX, NA)
    density = jnp.exp(jax.random.uniform(key_density, grid_shape, jnp.float32, math.log(0.5), math.log(2.0)))
    velocity = jnp.clip(0.5 * jax.random.normal(key_speed, (3,) + grid_shape, jnp.float32), -1.5, 1.5)
    pressure = jnp.exp(jax.random.uniform(key_pressure, grid_shape, jnp.float32, math.log(0.5), math.log(2.0)))
    momentum = density[None] * velocity
    energy = pressure / 0.4 + 0.5 * density * jnp.sum(velocity * velocity, axis=0)
    return jnp.concatenate([density[None], momentum, energy[None]], axis=0)


def draw_step_start(key, part):
    return flow_state(jax.random.fold_in(key, 11))


def draw_section_state(key, part):
    return flow_state(jax.random.fold_in(key, 23))


def draw_gore_map(key, part):
    key_twist, key_gap = jax.random.split(jax.random.fold_in(key, 37))
    station = jnp.arange(NX, dtype=jnp.int32)[:, None]
    column = jnp.arange(NA, dtype=jnp.int32)[None, :]
    twist = jax.random.randint(key_twist, (NX, 1), 0, GORES)
    gap_rows = (jax.random.randint(key_gap, (NX, 1), 0, 4) == 0) | (station == NX // 2)
    owner = (column * GORES // NA + twist) % GORES
    return jnp.where(gap_rows, GORES, owner).astype(jnp.int32)


def with_ends(entries, rng, low, top_value):
    longest = entries.shape.index(max(entries.shape))
    spots = []
    for shift in (0, 1):
        where = [jax.random.randint(jax.random.fold_in(rng, axis), (), 0, length) for axis, length in enumerate(entries.shape)]
        where[longest] = (where[longest] + shift) % entries.shape[longest]
        spots.append(tuple(where))
    return entries.at[spots[0]].set(low).at[spots[1]].set(top_value)


def setup_inputs(seed: int = 0) -> dict:
    seeds = jax.random.split(jax.random.key(seed), 6)
    return {
        "step_start": draw_step_start(jax.random.fold_in(seeds[5], 71), 0),
        "section_state": draw_section_state(jax.random.fold_in(seeds[5], 71), 0),
        "near_rows": with_ends(jax.random.randint(seeds[2], (NX,), 1, NF + 1), jax.random.fold_in(seeds[2], 1), 1, NF).astype(jnp.int32),
        "cutoff": with_ends(jax.random.randint(seeds[3], (NF, NX), NA // 32, NA // 4), jax.random.fold_in(seeds[3], 1), NA // 32, (NA // 4) - 1).astype(jnp.int32),
        "gore_map": draw_gore_map(jax.random.fold_in(seeds[5], 71), 0),
    }


HEAT_RATIO = 1.4
WEIGHT_EPSILON = 1e-06
INNER_RADIUS = 24.0
RADIAL_STEP = 0.5
AXIAL_STEP = 0.5
TIME_STEP = 0.01
SECTION_KEEP = 1.0 / 3.0
SECTION_GAIN = 2.0 / 3.0

def slice_along(values, along_dim, start_at, length):
    return lax.slice_in_dim(values, start_at, start_at + length, axis=along_dim)

def pressure_of(conserved):
    density = conserved[0]
    kinetic = 0.5 * (conserved[1] * conserved[1] + conserved[2] * conserved[2] + conserved[3] * conserved[3]) / density
    return (HEAT_RATIO - 1.0) * (conserved[4] - kinetic)

def cell_fluxes(conserved, normal):
    density = conserved[0]
    velocity = conserved[normal] / density
    pressure = pressure_of(conserved)
    flux_parts = [conserved[0] * velocity, conserved[1] * velocity, conserved[2] * velocity, conserved[3] * velocity, (conserved[4] + pressure) * velocity]
    flux_parts[normal] = flux_parts[normal] + pressure
    wave_speed = jnp.abs(velocity) + jnp.sqrt(HEAT_RATIO * pressure / density)
    return (jnp.stack(flux_parts), wave_speed)

def weno_side(far_left, near_left, centre, near_right, far_right):
    cand_one = (2.0 * far_left - 7.0 * near_left + 11.0 * centre) / 6.0
    cand_two = (-near_left + 5.0 * centre + 2.0 * near_right) / 6.0
    cand_three = (2.0 * centre + 5.0 * near_right - far_right) / 6.0
    smooth_one = 13.0 / 12.0 * jnp.square(far_left - 2.0 * near_left + centre) + 0.25 * jnp.square(far_left - 4.0 * near_left + 3.0 * centre)
    smooth_two = 13.0 / 12.0 * jnp.square(near_left - 2.0 * centre + near_right) + 0.25 * jnp.square(near_left - near_right)
    smooth_three = 13.0 / 12.0 * jnp.square(centre - 2.0 * near_right + far_right) + 0.25 * jnp.square(3.0 * centre - 4.0 * near_right + far_right)
    weight_one = 0.1 / jnp.square(WEIGHT_EPSILON + smooth_one)
    weight_two = 0.6 / jnp.square(WEIGHT_EPSILON + smooth_two)
    weight_three = 0.3 / jnp.square(WEIGHT_EPSILON + smooth_three)
    weight_sum = weight_one + weight_two + weight_three
    return (weight_one * cand_one + weight_two * cand_two + weight_three * cand_three) / weight_sum

def face_fluxes(padded, along_dim, normal):
    face_count = padded.shape[along_dim] - 5
    flux_cells, wave_speed = cell_fluxes(padded, normal)
    damping = jnp.maximum(slice_along(wave_speed, along_dim - 1, 2, face_count), slice_along(wave_speed, along_dim - 1, 3, face_count))[None]

    def plus_part(offset):
        return 0.5 * (slice_along(flux_cells, along_dim, 2 + offset, face_count) + damping * slice_along(padded, along_dim, 2 + offset, face_count))

    def minus_part(offset):
        return 0.5 * (slice_along(flux_cells, along_dim, 2 + offset, face_count) - damping * slice_along(padded, along_dim, 2 + offset, face_count))
    return weno_side(plus_part(-2), plus_part(-1), plus_part(0), plus_part(1), plus_part(2)) + weno_side(minus_part(3), minus_part(2), minus_part(1), minus_part(0), minus_part(-1))

def cell_difference(face_values, along_dim):
    cell_count = face_values.shape[along_dim] - 1
    return slice_along(face_values, along_dim, 1, cell_count) - slice_along(face_values, along_dim, 0, cell_count)

def rate_of(cycle_padded, line_padded):
    interior = cycle_padded[:, :, :, 3:-3]
    row_count = interior.shape[1]
    radial_padded = jnp.pad(interior, ((0, 0), (3, 3), (0, 0), (0, 0)), mode='edge')
    face_radius = INNER_RADIUS + RADIAL_STEP * jnp.arange(row_count + 1, dtype=jnp.float32)
    cell_radius = INNER_RADIUS + RADIAL_STEP * (jnp.arange(row_count, dtype=jnp.float32) + 0.5)
    radial_faces = face_fluxes(radial_padded, 1, 1) * face_radius[None, :, None, None]
    radial_term = cell_difference(radial_faces, 1) / (RADIAL_STEP * cell_radius)[None, :, None, None]
    cycle_term = cell_difference(face_fluxes(cycle_padded, 3, 2), 3) / (cell_radius * (2.0 * math.pi / NA))[None, :, None, None]
    line_term = cell_difference(face_fluxes(line_padded, 2, 3), 2) / AXIAL_STEP
    pressure = pressure_of(interior)
    swirl_speed = interior[2] / interior[0]
    radius_cells = cell_radius[:, None, None]
    source_radial = (interior[2] * swirl_speed + pressure) / radius_cells
    source_swirl = -interior[1] * swirl_speed / radius_cells
    zero_field = jnp.zeros_like(pressure)
    sources = jnp.stack([zero_field, source_radial, source_swirl, zero_field, zero_field])
    return (interior, sources - radial_term - cycle_term - line_term)

def reference(step_start, section_state, near_rows, cutoff, gore_map):
    padded = jnp.pad(section_state, ((0, 0), (0, 0), (3, 3), (0, 0)), mode='edge')
    padded = jnp.pad(padded, ((0, 0), (0, 0), (0, 0), (3, 3)), mode='wrap')
    block_rows = 16
    block_count = NX // block_rows

    def one_block(block_index):
        first_row = block_index * block_rows
        slab_block = lax.dynamic_slice_in_dim(padded, first_row, block_rows + 6, axis=2)
        interior, tendency = rate_of(slab_block[:, :, 3:-3, :], slab_block[:, :, :, 3:-3])
        start_block = lax.dynamic_slice_in_dim(step_start, first_row, block_rows, axis=2)
        return SECTION_KEEP * start_block + SECTION_GAIN * (interior + TIME_STEP * tendency)
    blocks = lax.map(one_block, jnp.arange(block_count, dtype=jnp.int32))
    updated = jnp.moveaxis(blocks, 0, 2).reshape(5, NR, NX, NA)
    near_cycles = updated[:, :NF]
    spectrum = jnp.fft.rfft(near_cycles, axis=-1)
    mode_index = jnp.arange(NA // 2 + 1, dtype=jnp.int32)
    kept_modes = mode_index[None, None, :] < cutoff[:, :, None]
    smoothed = jnp.fft.irfft(jnp.where(kept_modes[None], spectrum, 0.0), n=NA, axis=-1)
    chosen = jnp.arange(NF, dtype=jnp.int32)[:, None] < near_rows[None, :]
    near_new = jnp.where(chosen[None, :, :, None], smoothed, near_cycles)
    new_state = jnp.concatenate([near_new, updated[:, NF:]], axis=1)
    canopy = NR // 2
    pressure_jump = pressure_of(section_state[:, canopy - 1]) - pressure_of(section_state[:, canopy + 1])
    axial_ramp = 1.0 + 2.0 * jnp.arange(NX, dtype=jnp.float32) / NX
    weighted = pressure_jump * axial_ramp[:, None] * (1.0 / math.sqrt(NX * NA / GORES))
    gore_loads = jax.ops.segment_sum(weighted.reshape(-1), gore_map.reshape(-1), num_segments=GORES + 1)[:GORES]
    return (new_state, gore_loads)
```

```python
import functools
import math

import jax
import jax.numpy as jnp
import numpy as np
from jax import lax
from jax.experimental import pallas as pl
from jax.experimental.pallas import tpu as pltpu
from jax.sharding import PartitionSpec as P

NA = 2048
NF = 4
GORES = 80

HEAT_RATIO = 1.4
WEIGHT_EPSILON = 1e-06
INNER_RADIUS = 24.0
RADIAL_STEP = 0.5
AXIAL_STEP = 0.5
TIME_STEP = 0.01
SECTION_KEEP = 1.0 / 3.0
SECTION_GAIN = 2.0 / 3.0

SB = 8
EPS = 3.0 * WEIGHT_EPSILON


def side(d1, d2, d3, d4):
    e1 = d2 - d1
    e2 = d3 - d2
    e3 = d4 - d3
    h2 = 0.75 * d2
    h3 = 0.75 * d3
    g2 = h2 * d2 + EPS
    g3 = h3 * d3 + EPS
    s1 = e1 * (e1 + h2) + g2
    s2 = e2 * (e2 + h2) + g2
    s3 = e3 * (e3 - h3) + g3
    t1 = s2 * pl.reciprocal(s1, approx=False)
    t3 = s2 * pl.reciprocal(s3, approx=False)
    w1 = t1 * t1
    w3 = 3.0 * (t3 * t3)
    num = (w1 + w1) * (e1 - e2) + w3 * (e2 - e3)
    return num * pl.reciprocal((w1 + 6.0) + w3, approx=False), e2


def face_flux12(df, du, a, fsum):
    au = [a * x for x in du]
    pm2, pm1, p0, p1 = (df[k] + au[k] for k in range(4))
    mm1, m0, m1, m2 = (df[k] - au[k] for k in range(1, 5))
    cp, ep = side(pm2, pm1, p0, p1)
    cm, em = side(m2, m1, m0, mm1)
    return 6.0 * fsum + ((cp - cm) - (ep - em))


def primitives(u):
    rinv = 1.0 / u[0]
    kin = 0.5 * (u[1] * u[1] + u[2] * u[2] + u[3] * u[3]) * rinv
    p = (HEAT_RATIO - 1.0) * (u[4] - kin)
    cs = jnp.sqrt(HEAT_RATIO * p * rinv)
    return rinv, p, cs


def fluxes(u, vel, p, normal):
    f = [u[normal], u[1] * vel, u[2] * vel, u[3] * vel, (u[4] + p) * vel]
    f[normal] = f[normal] + p
    return f


def tiles(ref, *ix):
    cells = ref.shape[-1]
    return jnp.stack([ref[(*ix, slice(128 * l, 128 * l + 128))] for l in range(cells // 128)])


def radial_kernel(rows, lt, state, start, part, DR, SR, RF, LF, S1, S2):
    i = pl.program_id(0)
    every = slice(None)

    @pl.when(i == 0)
    def _():
        for e in (0, 1, 2, rows + 2, rows + 3, rows + 4):
            DR[:, :, e] = jnp.zeros((5, 2, lt, SB, 128), jnp.float32)

    def cell(q):
        u = [tiles(state, c, q, every) for c in range(5)]
        rinv, p, cs = primitives(u)
        vel = u[1] * rinv
        swirl = u[2] * rinv
        S1[q] = u[2] * swirl + p
        S2[q] = u[1] * swirl
        return u, fluxes(u, vel, p, 1), jnp.abs(vel) + cs

    def edge(e, carry):
        u, f, s = carry[:5], carry[5:10], carry[10]
        un, fn, sn = cell(e - 2)
        for c in range(5):
            DR[c, 0, e] = fn[c] - f[c]
            DR[c, 1, e] = un[c] - u[c]
            RF[c, e] = fn[c] + f[c]
        SR[e] = jnp.maximum(s, sn)
        return (*un, *fn, sn)

    u, f, s = cell(0)
    for c in range(5):
        RF[c, 2] = f[c] + f[c]
    SR[2] = s
    last = lax.fori_loop(3, rows + 2, edge, (*u, *f, s))
    for c in range(5):
        RF[c, rows + 2] = last[5 + c] + last[5 + c]
    SR[rows + 2] = last[10]

    def face(c, e):
        df = [DR[c, 0, e + k] for k in range(-2, 3)]
        du = [DR[c, 1, e + k] for k in range(-2, 3)]
        return face_flux12(df, du, SR[e], RF[c, e])

    for c in range(5):
        LF[c] = face(c, 2)
    gain = SECTION_GAIN * TIME_STEP

    def one_row(r, _):
        row = r.astype(jnp.float32)
        radius = INNER_RADIUS + RADIAL_STEP * (row + 0.5)
        rr = 1.0 / jnp.full((1, 1, 128), radius, jnp.float32)
        k_low = (gain / 12.0 / RADIAL_STEP) * (INNER_RADIUS + RADIAL_STEP * row) * rr
        k_up = (gain / 12.0 / RADIAL_STEP) * (INNER_RADIUS + RADIAL_STEP * (row + 1.0)) * rr
        k_src = gain * rr
        for c in range(5):
            up = face(c, r + 3)
            value = k_low * LF[c] - k_up * up
            LF[c] = up
            value = value + (SECTION_KEEP * tiles(start, c, r, every) + SECTION_GAIN * tiles(state, c, r, every))
            if c == 1:
                value = value + k_src * S1[r]
            if c == 2:
                value = value - k_src * S2[r]
            for l in range(lt):
                part[c, r, :, 128 * l:128 * l + 128] = value[l]
        return 0

    lax.fori_loop(0, rows, one_row, 0)


def radial_part(state, start):
    _, rows, stations, cells = state.shape
    lt = cells // 128
    f32 = jnp.float32
    spec = pl.BlockSpec((5, rows, SB, cells), lambda i: (0, 0, i, 0))
    return pl.pallas_call(
        functools.partial(radial_kernel, rows, lt),
        out_shape=jax.ShapeDtypeStruct(state.shape, f32),
        grid=(stations // SB,),
        in_specs=[spec, spec],
        out_specs=spec,
        scratch_shapes=[
            pltpu.VMEM((5, 2, rows + 5, lt, SB, 128), f32),
            pltpu.VMEM((rows + 5, lt, SB, 128), f32),
            pltpu.VMEM((5, rows + 5, lt, SB, 128), f32),
            pltpu.VMEM((5, lt, SB, 128), f32),
            pltpu.VMEM((rows, lt, SB, 128), f32),
            pltpu.VMEM((rows, lt, SB, 128), f32),
        ],
        compiler_params=pltpu.CompilerParams(
            dimension_semantics=("arbitrary",), vmem_limit_bytes=48 << 20),
        cost_estimate=pl.CostEstimate(
            flops=state.size * 90, bytes_accessed=state.size * 12, transcendentals=0),
        name="radial_part",
    )(state, start)


def rows_kernel(cfg, *refs):
    r0, lt, nblk, share = cfg
    state, ahead, lo, hi, left, right, part = refs[:7]
    out = refs[-15]
    U, F, DF, DU, FF, SX, UZ, FZ, DFZ, DUZ, FFZ, SZ, TZ, AZ = refs[-14:]
    st = nblk * SB
    cells = lt * 128
    nz = cells // SB
    step = 2 * SB
    turns = cells // step
    per_turn = nblk // turns
    per_line = nz // nblk
    i = pl.program_id(0)
    lr = i + r0
    every = slice(None)
    sub = lax.broadcasted_iota(jnp.int32, (SB, 128), 0)

    line = lax.axis_index("ax")
    at_low = line == 0
    at_high = line == lax.axis_size("ax") - 1

    def block(b):
        return pl.ds(b * SB if isinstance(b, int) else pl.multiple_of(b * SB, SB), SB)

    def line_cells(u, b):
        rinv, p, cs = primitives(u)
        vel = u[3] * rinv
        f = fluxes(u, vel, p, 3)
        ds = block(b)
        for c in range(5):
            U[c, :, ds, :] = u[c]
            F[c, :, ds, :] = f[c]
        SX[:, ds, :] = jnp.abs(vel) + cs

    def line_end(ref, at_end, b, edge, to):
        u = []
        for c in range(5):
            inner = tiles(state, c, block(b))[:, edge:edge + 1]
            u.append(jnp.where(at_end, jnp.broadcast_to(inner, (lt, SB, 128)), tiles(ref, c, every)))
        line_cells(u, to)

    def line_block(b):
        line_cells([tiles(state, c, block(b)) for c in range(5)], b + 1)

    def turned_tile(src, t):
        c, l = t // lt, t % lt
        at = 128 * l
        if not isinstance(t, int):
            at = pl.multiple_of(at, 128)
        UZ[c, 0, pl.ds(at + SB, 128), :] = src[c, :, pl.ds(at, 128)].T

    def cycle_ends(row):
        for c in range(5):
            UZ[c, 0, pl.ds(0, SB), :] = pltpu.roll(left[c, block(row), :], 5, 0)
            UZ[c, 0, pl.ds(SB + cells, SB), :] = pltpu.roll(right[c, block(row), :], 5, 0)

    def cycle_cells(b):
        ds = block(b)
        u = [UZ[c, :, ds, :] for c in range(5)]
        rinv, p, cs = primitives(u)
        vel = u[2] * rinv
        f = fluxes(u, vel, p, 2)
        for c in range(5):
            FZ[c, :, ds, :] = f[c]
        SZ[:, ds, :] = jnp.abs(vel) + cs

    lines = ((F, DF), (U, DU))
    cycles = ((FZ, DFZ), (UZ, DUZ))

    def diff_block(pairs, b):
        o = b * SB if isinstance(b, int) else pl.multiple_of(b * SB, SB)
        for X, D in pairs:
            for c in range(5):
                D[c, :, pl.ds(o, SB), :] = X[c, :, pl.ds(o + 1, SB), :] - X[c, :, pl.ds(o, SB), :]

    def diff_last(pairs, b):
        for X, D in pairs:
            for c in range(5):
                x = X[c, :, block(b), :]
                D[c, :, block(b), :] = pltpu.roll(x, SB - 1, 1) - x

    def faces(F, DF, DU, S, c, base, n):
        df = [DF[c, :, pl.ds(base + k, n), :] for k in range(-2, 3)]
        du = [DU[c, :, pl.ds(base + k, n), :] for k in range(-2, 3)]
        a = jnp.maximum(S[:, pl.ds(base, n), :], S[:, pl.ds(base + 1, n), :])
        return face_flux12(df, du, a, F[c, :, pl.ds(base, n), :] + F[c, :, pl.ds(base + 1, n), :])

    def first_faces(F, DF, DU, S, FF):
        e = SB - 1
        for l in range(F.shape[1]):
            def pick(X, k):
                x = X[0, l, pl.ds(e + k, SB), :]
                for c in range(1, 5):
                    x = jnp.where(sub == c, X[c, l, pl.ds(e + k - c, SB), :], x)
                return x

            df = [pick(DF, k) for k in range(-2, 3)]
            du = [pick(DU, k) for k in range(-2, 3)]
            a = jnp.maximum(S[l, pl.ds(e, 1), :], S[l, pl.ds(e + 1, 1), :])
            f = face_flux12(df, du, a, pick(F, 0) + pick(F, 1))
            for c in range(5):
                FF[c, l, pl.ds(e, 1), :] = f[c:c + 1]

    gain = SECTION_GAIN * TIME_STEP
    radius = INNER_RADIUS + RADIAL_STEP * (lr.astype(jnp.float32) + 0.5)
    rr = 1.0 / jnp.full((1, 1, 128), radius, jnp.float32)
    k_cycle = (gain / 12.0 * NA / (2.0 * math.pi)) * rr
    k_line = gain / 12.0 / AXIAL_STEP

    @pl.when(i == 0)
    def _():
        for t in range(5 * lt):
            turned_tile(state, t)
        cycle_ends(lr)

        def cells_loop(b, _):
            cycle_cells(b)
            return 0

        def diff_loop(b, _):
            diff_block(cycles, b)
            return 0

        lax.fori_loop(0, nz + 2, cells_loop, 0)
        lax.fori_loop(0, nz + 1, diff_loop, 0)
        diff_last(cycles, nz + 1)
        first_faces(FZ, DFZ, DUZ, SZ, FFZ)

    def cycle_turn(b, _):
        base = pl.multiple_of(b * step + SB, SB)
        for c in range(5):
            fa = faces(FZ, DFZ, DUZ, SZ, c, base, step)
            FFZ[c, :, pl.ds(base, step), :] = fa
            TZ[c, pl.ds(pl.multiple_of(b * step, step), step), :] = (
                k_cycle * (FFZ[c, :, pl.ds(base - 1, step), :] - fa))[0]
        for j in range(per_turn):
            diff_block(lines, jnp.maximum(per_turn * b - per_turn + j, 0))
        for j in range(per_turn):
            line_block(per_turn * b + j)
        turned_tile(ahead, jnp.minimum(b, 5 * lt - 1))
        return 0

    lax.fori_loop(0, turns, cycle_turn, 0)

    line_end(lo, at_low, 0, 0, 0)
    line_end(hi, at_high, nblk - 1, SB - 1, nblk + 1)
    diff_block(lines, 0)
    for b in range(nblk - per_turn, nblk + 1):
        diff_block(lines, b)
    diff_last(lines, nblk + 1)
    first_faces(F, DF, DU, SX, FF)
    for c in range(5):
        for l in range(lt):
            AZ[c, l] = TZ[c, pl.ds(128 * l, 128), :].T
    cycle_ends(jnp.minimum(lr + 1, r0 + pl.num_programs(0) - 1))

    def line_turn(b, _):
        hs = block(b)
        base = pl.multiple_of(b * SB + SB, SB)
        for c in range(5):
            fx = faces(F, DF, DU, SX, c, base, SB)
            FF[c, :, pl.ds(base, SB), :] = fx
            delta = k_line * (FF[c, :, pl.ds(base - 1, SB), :] - fx) + AZ[c, :, hs, :]
            for l in range(lt):
                ls = slice(128 * l, 128 * l + 128)
                value = part[c, hs, ls] + delta[l]
                if share:
                    at = b * SB
                    out[at // share, c, pl.ds(pl.multiple_of(at % share, SB), SB), ls] = value
                else:
                    out[c, hs, ls] = value
        for j in range(per_line):
            diff_block(cycles, jnp.maximum(per_line * b - per_line - 1 + j, 0))
        for j in range(per_line):
            cycle_cells(per_line * b + j)
        return 0

    lax.fori_loop(0, nblk, line_turn, 0)

    cycle_cells(nz)
    cycle_cells(nz + 1)
    for b in range(nz - per_line - 1, nz + 1):
        diff_block(cycles, b)
    diff_last(cycles, nz + 1)
    first_faces(FZ, DFZ, DUZ, SZ, FFZ)


def rk_rows(state, lo, hi, left, right, part, r0, r1, share=0, into=None):
    _, rows, stations, cells = state.shape
    lt = cells // 128
    nblk = stations // SB
    f32 = jnp.float32
    any_spec = pl.BlockSpec(memory_space=pl.ANY)
    row_spec = pl.BlockSpec((5, None, stations, cells), lambda i: (0, i + r0, 0, 0))
    end_spec = pl.BlockSpec((5, None, SB, cells), lambda i: (0, i + r0, 0, 0))
    pack_spec = pl.BlockSpec((5, rows * 8, stations), lambda i: (0, 0, 0))
    ahead_spec = pl.BlockSpec(
        (5, None, stations, cells), lambda i: (0, jnp.minimum(i + r0 + 1, r1 - 1), 0, 0))
    in_specs = [row_spec, ahead_spec, end_spec, end_spec, pack_spec, pack_spec, row_spec]
    args = [state, state, lo, hi, left, right, part]
    alias = {}
    if share:
        groups = stations // share
        out_shape = jax.ShapeDtypeStruct((groups, 5, r1 - r0, share, cells), f32)
        out_spec = pl.BlockSpec((groups, 5, None, share, cells), lambda i: (0, 0, i, 0, 0))
    else:
        if into is not None:
            in_specs.append(any_spec)
            args.append(into)
            alias = {7: 0}
        out_shape, out_spec = jax.ShapeDtypeStruct(state.shape, f32), row_spec
    field = pltpu.VMEM((lt, stations + 2 * SB, 128), f32)
    group = pltpu.VMEM((5, lt, stations + 2 * SB, 128), f32)
    field_z = pltpu.VMEM((1, cells + 2 * SB, stations), f32)
    group_z = pltpu.VMEM((5, 1, cells + 2 * SB, stations), f32)
    return pl.pallas_call(
        functools.partial(rows_kernel, (r0, lt, nblk, share)),
        out_shape=out_shape,
        grid=(r1 - r0,),
        in_specs=in_specs,
        out_specs=out_spec,
        scratch_shapes=[group] * 5 + [field] + [group_z] * 5 + [
            field_z,
            pltpu.VMEM((5, cells, stations), f32),
            pltpu.VMEM((5, lt, stations, 128), f32),
        ],
        input_output_aliases=alias,
        compiler_params=pltpu.CompilerParams(
            dimension_semantics=("arbitrary",), vmem_limit_bytes=56 << 20),
        cost_estimate=pl.CostEstimate(
            flops=5 * (r1 - r0) * stations * cells * 180,
            bytes_accessed=5 * (r1 - r0) * stations * cells * 12, transcendentals=0),
        name="rk_rows_%d_%d" % (r0, r1),
    )(*args)


def place_kernel(final, whole, out):
    groups, _, share, cells = final.shape
    for g in range(groups):
        out[:, g * share:(g + 1) * share, :] = final[g]


def place_near(final, whole):
    groups, _, _, share, cells = final.shape
    return pl.pallas_call(
        place_kernel,
        out_shape=jax.ShapeDtypeStruct(whole.shape, jnp.float32),
        grid=(NF,),
        in_specs=[pl.BlockSpec((groups, 5, None, share, cells), lambda i: (0, 0, i, 0, 0)),
                  pl.BlockSpec(memory_space=pl.ANY)],
        out_specs=pl.BlockSpec((5, None, groups * share, cells), lambda i: (0, i, 0, 0)),
        input_output_aliases={1: 0},
        compiler_params=pltpu.CompilerParams(vmem_limit_bytes=60 << 20),
        name="place_near",
    )(final, whole)


def edge_kernel(head, tail, out):
    rows = head.shape[0]
    lane = lax.broadcasted_iota(jnp.int32, head.shape[1:], 1)
    acc = jnp.zeros(head.shape[1:], jnp.float32)
    for r in range(rows):
        ends = jnp.where(lane < 64, head[r], tail[r])
        ends = pltpu.roll(ends, (8 * r + 3) % 128, 1)
        acc = jnp.where((lane >= 8 * r) & (lane < 8 * r + 8), ends, acc)
    out[...] = acc.T


def azimuthal_edges(state):
    _, rows, stations, cells = state.shape
    far = cells // 128 - 1
    return pl.pallas_call(
        edge_kernel,
        out_shape=jax.ShapeDtypeStruct((5, rows * 8, stations), jnp.float32),
        grid=(5,),
        in_specs=[pl.BlockSpec((None, rows, stations, 128), lambda i: (i, 0, 0, 0)),
                  pl.BlockSpec((None, rows, stations, 128), lambda i: (i, 0, 0, far))],
        out_specs=pl.BlockSpec((None, rows * 8, stations), lambda i: (i, 0, 0)),
        name="azimuthal_edges",
    )(state, state)


def mode_tables():
    n = np.arange(NA // 2)[:, None]
    tables = []
    for parity in (0, 1):
        k = np.arange(parity, NA // 4, 2)[None, :]
        angle = 2.0 * math.pi / NA * ((n * k) % NA)
        table = np.concatenate([np.cos(angle), np.sin(angle)], axis=1).astype(np.float32)
        high = table.astype(jnp.bfloat16)
        tables += [high, (table - high.astype(np.float32)).astype(jnp.bfloat16)]
    return tables


def split(x):
    high = x.astype(jnp.bfloat16)
    return high, (x - high.astype(jnp.float32)).astype(jnp.bfloat16)


def product(x, y, dims):
    x_high, x_low = x
    y_high, y_low = y

    def dot(a, b):
        return lax.dot_general(a, b, (dims, ((), ())), preferred_element_type=jnp.float32)

    return dot(x_high, y_high) + (dot(x_low, y_high) + dot(x_high, y_low))


def low_pass_kernel(x, signed, even_high, even_low, odd_high, odd_low, out):
    pieces, _, _, share, cells = x.shape
    m = 5 * NF * share
    half = pieces // 2
    tables = ((even_high, even_low), (odd_high, odd_low))
    modes = even_high.shape[1] // 2
    coef = [0.0, 0.0]
    for p in range(half):
        x0 = x[p].reshape(m, cells)
        x1 = x[p + half].reshape(m, cells)
        at = slice(p * cells, (p + 1) * cells)
        for parity, part in enumerate((x0 + x1, x0 - x1)):
            rhs = tuple(t[at, :] for t in tables[parity])
            coef[parity] = coef[parity] + product(split(part), rhs, ((1,), (0,)))
    signed = jnp.concatenate([signed[...]] * 5, axis=0)
    limit = jnp.abs(signed)
    take = signed > 0
    column = lax.broadcasted_iota(jnp.int32, (m, 2 * modes), 1)
    column = jnp.where(column < modes, column, column - modes)
    back = []
    for parity in range(2):
        k = 2 * column + parity
        weight = jnp.where(k == 0, 1.0 / NA, 2.0 / NA)
        gains = jnp.where(k < limit, weight, 0.0)
        back.append(split(coef[parity] * gains))
    for p in range(half):
        at = slice(p * cells, (p + 1) * cells)
        y0, y1 = (
            product(back[parity], tuple(t[at, :] for t in tables[parity]), ((1,), (1,)))
            for parity in range(2)
        )
        for q, y in ((p, y0 + y1), (p + half, y0 - y1)):
            kept = jnp.where(take, y, x[q].reshape(m, cells))
            out[q] = kept.reshape(5, NF, share, cells)


def low_pass(cycles, cutoffs, rows_here):
    share = cycles.shape[3]
    chosen = jnp.arange(NF, dtype=jnp.int32)[:, None] < rows_here[None, :]
    limit = jnp.where(chosen, cutoffs, -cutoffs).reshape(NF * share, 1)
    tables = [jnp.asarray(t) for t in mode_tables()]
    return pl.pallas_call(
        low_pass_kernel,
        out_shape=jax.ShapeDtypeStruct(cycles.shape, jnp.float32),
        compiler_params=pltpu.CompilerParams(vmem_limit_bytes=60 << 20),
        name="low_pass",
    )(cycles, limit, *tables)


def pressure_of(conserved):
    density = conserved[0]
    kinetic = (
        0.5
        * (conserved[1] * conserved[1] + conserved[2] * conserved[2] + conserved[3] * conserved[3])
        / density
    )
    return (HEAT_RATIO - 1.0) * (conserved[4] - kinetic)


def per_device(step_start, section_state, near_rows, cutoff, gore_map):
    _, rows, stations, cells = section_state.shape
    na, nx = lax.axis_size("az"), lax.axis_size("ax")
    cycle_index, line_index = lax.axis_index("az"), lax.axis_index("ax")
    up_a = [(i, (i + 1) % na) for i in range(na)]
    down_a = [((i + 1) % na, i) for i in range(na)]
    up_x = [(i, (i + 1) % nx) for i in range(nx)]
    down_x = [((i + 1) % nx, i) for i in range(nx)]

    edges = azimuthal_edges(section_state)
    left = lax.ppermute(edges, "az", up_a)
    right = lax.ppermute(edges, "az", down_a)
    lo = lax.ppermute(section_state[:, :, -SB:], "ax", up_x)
    hi = lax.ppermute(section_state[:, :, :SB], "ax", down_x)

    canopy = rows // 2
    jump = pressure_of(section_state[:, canopy - 1]) - pressure_of(section_state[:, canopy + 1])
    total = stations * nx
    station = line_index * stations + jnp.arange(stations, dtype=jnp.int32)
    ramp = 1.0 + 2.0 * station.astype(jnp.float32) / total
    weighted = jump * ramp[:, None] * (1.0 / math.sqrt(total * NA / GORES))
    gores = jnp.arange(GORES, dtype=jnp.int32)
    partial = jnp.sum(
        jnp.where(gore_map[None] == gores[:, None, None], weighted[None], 0.0), axis=(1, 2))
    parts = jnp.broadcast_to(jnp.pad(partial, (0, 128 - GORES)), (na * nx, 128))
    parts = lax.all_to_all(parts, ("az", "ax"), 0, 0, tiled=True)

    part = radial_part(section_state, step_start)
    part, parts, left, right, lo, hi = lax.optimization_barrier(
        (part, parts, left, right, lo, hi))
    rest = functools.partial(rk_rows, section_state, lo, hi, left, right, part)
    share = stations // na
    near = rest(0, NF, share=share)
    spread = lax.all_to_all(near, "az", 0, 0, tiled=True)
    middle = NF + (rows - NF) // 2
    whole = rest(NF, middle)
    spread, whole = lax.optimization_barrier((spread, whole))
    cutoffs = lax.dynamic_slice_in_dim(cutoff, cycle_index * share, share, axis=1)
    rows_here = lax.dynamic_slice_in_dim(near_rows, cycle_index * share, share, axis=0)
    kept = low_pass(spread, cutoffs, rows_here)
    kept, whole = lax.optimization_barrier((kept, whole))
    final = lax.all_to_all(kept, "az", 0, 0, tiled=True)
    whole = rest(middle, rows, into=whole)

    new_state = place_near(final, whole)
    return (new_state, jnp.sum(parts, axis=0)[:GORES])


def solution(mesh):
    in_specs = (
        P(None, None, "ax", "az"),
        P(None, None, "ax", "az"),
        P("ax"),
        P(None, "ax"),
        P("ax", "az"),
    )
    out_specs = (P(None, None, "ax", "az"), P())
    return jax.shard_map(
        per_device, mesh=mesh, in_specs=in_specs, out_specs=out_specs, check_vma=False
    )
```

```python
import functools
import math

import jax
import jax.numpy as jnp
import numpy as np
from jax import lax
from jax.experimental import pallas as pl
from jax.experimental.pallas import tpu as pltpu
from jax.sharding import PartitionSpec as P

NA = 2048
NF = 4
GORES = 80

HEAT_RATIO = 1.4
WEIGHT_EPSILON = 1e-06
INNER_RADIUS = 24.0
RADIAL_STEP = 0.5
AXIAL_STEP = 0.5
TIME_STEP = 0.01
SECTION_KEEP = 1.0 / 3.0
SECTION_GAIN = 2.0 / 3.0

SB = 8
EPS = 3.0 * WEIGHT_EPSILON


def side(d1, d2, d3, d4):
    e1 = d2 - d1
    e2 = d3 - d2
    e3 = d4 - d3
    h2 = 0.75 * d2
    h3 = 0.75 * d3
    g2 = h2 * d2 + EPS
    g3 = h3 * d3 + EPS
    s1 = e1 * (e1 + h2) + g2
    s2 = e2 * (e2 + h2) + g2
    s3 = e3 * (e3 - h3) + g3
    t1 = s2 * pl.reciprocal(s1, approx=False)
    t3 = s2 * pl.reciprocal(s3, approx=False)
    w1 = t1 * t1
    w3 = 3.0 * (t3 * t3)
    num = (w1 + w1) * (e1 - e2) + w3 * (e2 - e3)
    return num * pl.reciprocal((w1 + 6.0) + w3, approx=False), e2


def face_flux12(df, du, a, fsum):
    au = [a * x for x in du]
    pm2, pm1, p0, p1 = (df[k] + au[k] for k in range(4))
    mm1, m0, m1, m2 = (df[k] - au[k] for k in range(1, 5))
    cp, ep = side(pm2, pm1, p0, p1)
    cm, em = side(m2, m1, m0, mm1)
    return 6.0 * fsum + ((cp - cm) - (ep - em))


def primitives(u):
    rinv = 1.0 / u[0]
    kin = 0.5 * (u[1] * u[1] + u[2] * u[2] + u[3] * u[3]) * rinv
    p = (HEAT_RATIO - 1.0) * (u[4] - kin)
    cs = jnp.sqrt(HEAT_RATIO * p * rinv)
    return rinv, p, cs


def fluxes(u, vel, p, normal):
    f = [u[normal], u[1] * vel, u[2] * vel, u[3] * vel, (u[4] + p) * vel]
    f[normal] = f[normal] + p
    return f


def tiles(ref, *ix):
    cells = ref.shape[-1]
    return jnp.stack([ref[(*ix, slice(128 * l, 128 * l + 128))] for l in range(cells // 128)])


def radial_kernel(rows, lt, na, nx, state, start, low_end, high_end, sums,
                  part, left, right, lo, hi, total,
                  DR, SR, RF, LF, S1, S2, pack, own, from_ax, from_az, line_sum,
                  end_send, end_recv, pack_send, pack_recv, ax_send, ax_recv, az_send, az_recv):
    i = pl.program_id(0)
    every = slice(None)
    me_a, me_x = lax.axis_index("az"), lax.axis_index("ax")
    nblk = pack.shape[0]
    per_step = rows // nblk
    assert per_step * nblk == rows
    MESH = pl.DeviceIdType.MESH

    def peer_a(d):
        return {"az": lax.rem(me_a + d, na)}

    def peer_x(d):
        return {"ax": lax.rem(me_x + d, nx)}

    def copy(src, dst, send, recv, peer):
        return pltpu.make_async_remote_copy(
            src_ref=src, dst_ref=dst, send_sem=send, recv_sem=recv,
            device_id=peer, device_id_type=MESH)

    def end_copies(r):
        return [
            copy(high_end.at[:, r], lo.at[:, r], end_send.at[0, r], end_recv.at[0, r], peer_x(1)),
            copy(low_end.at[:, r], hi.at[:, r], end_send.at[1, r], end_recv.at[1, r], peer_x(nx - 1)),
        ]

    def pack_copies(b):
        return [
            copy(pack.at[b], left.at[b], pack_send.at[0, b], pack_recv.at[0, b], peer_a(1)),
            copy(pack.at[b], right.at[b], pack_send.at[1, b], pack_recv.at[1, b], peer_a(na - 1)),
        ]

    def line_copies():
        return [
            copy(own, from_ax.at[me_x], ax_send.at[d], ax_recv.at[d], peer_x(d + 1))
            for d in range(nx - 1)
        ]

    def cycle_copies():
        return [
            copy(line_sum, from_az.at[me_a], az_send.at[d], az_recv.at[d], peer_a(d + 1))
            for d in range(na - 1)
        ]

    def ordered_sum(ref, count):
        value = ref[0]
        for d in range(1, count):
            value = value + ref[d]
        return value

    @pl.when(i == 0)
    def _():
        barrier = pltpu.get_barrier_semaphore()
        for d in range(1, na):
            pl.semaphore_signal(barrier, inc=1, device_id=peer_a(d), device_id_type=MESH)
        for d in range(1, nx):
            pl.semaphore_signal(barrier, inc=1, device_id=peer_x(d), device_id_type=MESH)
        own[...] = jnp.zeros((SB, 128), jnp.float32)
        own[0:1, 0:GORES] = sums[...].reshape(1, GORES)
        for e in (0, 1, 2, rows + 2, rows + 3, rows + 4):
            DR[:, :, e] = jnp.zeros((5, 2, lt, SB, 128), jnp.float32)

    @pl.when(i == 1)
    def _():
        pl.semaphore_wait(pltpu.get_barrier_semaphore(), na + nx - 2)
        for cp in line_copies():
            cp.start()

    @pl.when(i == nblk // 4)
    def _():
        for cp in line_copies():
            cp.wait()
        from_ax[me_x] = own[...]
        line_sum[...] = ordered_sum(from_ax, nx)
        for cp in cycle_copies():
            cp.start()

    lane = lax.broadcasted_iota(jnp.int32, (SB, 128), 1)
    near_side = lane < 64
    owner = lane // 8

    def cell(q):
        u = [tiles(state, c, q, every) for c in range(5)]
        rinv, p, cs = primitives(u)
        vel = u[1] * rinv
        swirl = u[2] * rinv
        S1[q] = u[2] * swirl + p
        S2[q] = u[1] * swirl
        return u, fluxes(u, vel, p, 1), jnp.abs(vel) + cs

    def edge(e, carry):
        u, f, s = carry[:5], carry[5:10], carry[10]
        un, fn, sn = cell(e - 2)
        for c in range(5):
            DR[c, 0, e] = fn[c] - f[c]
            DR[c, 1, e] = un[c] - u[c]
            RF[c, e] = fn[c] + f[c]
        SR[e] = jnp.maximum(s, sn)
        return (*un, *fn, sn)

    u, f, s = cell(0)
    for c in range(5):
        RF[c, 2] = f[c] + f[c]
    SR[2] = s
    last = lax.fori_loop(3, rows + 2, edge, (*u, *f, s))
    for c in range(5):
        RF[c, rows + 2] = last[5 + c] + last[5 + c]
    SR[rows + 2] = last[10]

    def face(c, e):
        df = [DR[c, 0, e + k] for k in range(-2, 3)]
        du = [DR[c, 1, e + k] for k in range(-2, 3)]
        return face_flux12(df, du, SR[e], RF[c, e])

    for c in range(5):
        value = None
        for q in range(rows):
            ends = jnp.where(near_side, state[c, q, :, 0:128], state[c, q, :, 128 * (lt - 1):128 * lt])
            ends = pltpu.roll(ends, (8 * q + 3) % 128, 1)
            value = ends if q == 0 else jnp.where(owner == q, ends, value)
        pack[i, c] = value
        LF[c] = face(c, 2)

    def send(b):
        for cp in pack_copies(b):
            cp.start()
        for j in range(per_step):
            for cp in end_copies(b * per_step + j):
                cp.start()

    @pl.when(i > 0)
    def _():
        send(i - 1)

    @pl.when(i == nblk - 1)
    def _():
        send(i)

    gain = SECTION_GAIN * TIME_STEP

    def one_row(r, _):
        row = r.astype(jnp.float32)
        radius = INNER_RADIUS + RADIAL_STEP * (row + 0.5)
        rr = 1.0 / jnp.full((1, 1, 128), radius, jnp.float32)
        k_low = (gain / 12.0 / RADIAL_STEP) * (INNER_RADIUS + RADIAL_STEP * row) * rr
        k_up = (gain / 12.0 / RADIAL_STEP) * (INNER_RADIUS + RADIAL_STEP * (row + 1.0)) * rr
        k_src = gain * rr
        for c in range(5):
            up = face(c, r + 3)
            value = k_low * LF[c] - k_up * up
            LF[c] = up
            value = value + (SECTION_KEEP * tiles(start, c, r, every) + SECTION_GAIN * tiles(state, c, r, every))
            if c == 1:
                value = value + k_src * S1[r]
            if c == 2:
                value = value - k_src * S2[r]
            for l in range(lt):
                part[c, r, :, 128 * l:128 * l + 128] = value[l]
        return 0

    lax.fori_loop(0, rows, one_row, 0)

    @pl.when(i == nblk - 1)
    def _():
        for cp in cycle_copies():
            cp.wait()
        from_az[me_a] = line_sum[...]
        total[...] = ordered_sum(from_az, na)

        def finish(b, _):
            for cp in pack_copies(b):
                cp.wait()
            for j in range(per_step):
                for cp in end_copies(b * per_step + j):
                    cp.wait()
            return 0

        lax.fori_loop(0, nblk, finish, 0)


def radial_part(state, start, sums, na, nx):
    _, rows, stations, cells = state.shape
    lt = cells // 128
    nblk = stations // SB
    f32 = jnp.float32
    spec = pl.BlockSpec((5, rows, SB, cells), lambda i: (0, 0, i, 0))
    low_spec = pl.BlockSpec((5, rows, SB, cells), lambda i: (0, 0, 0, 0))
    high_spec = pl.BlockSpec((5, rows, SB, cells), lambda i: (0, 0, nblk - 1, 0))
    small = pl.BlockSpec((SB, 128), lambda i: (0, 0))
    any_spec = pl.BlockSpec(memory_space=pl.ANY)
    side = jax.ShapeDtypeStruct((nblk, 5, SB, 128), f32)
    end = jax.ShapeDtypeStruct((5, rows, SB, cells), f32)
    dma = pltpu.SemaphoreType.DMA
    return pl.pallas_call(
        functools.partial(radial_kernel, rows, lt, na, nx),
        out_shape=(jax.ShapeDtypeStruct(state.shape, f32), side, side, end, end,
                   jax.ShapeDtypeStruct((SB, 128), f32)),
        grid=(nblk,),
        in_specs=[spec, spec, low_spec, high_spec, pl.BlockSpec((GORES,), lambda i: (0,))],
        out_specs=(spec,) + (any_spec,) * 4 + (small,),
        scratch_shapes=[
            pltpu.VMEM((5, 2, rows + 5, lt, SB, 128), f32),
            pltpu.VMEM((rows + 5, lt, SB, 128), f32),
            pltpu.VMEM((5, rows + 5, lt, SB, 128), f32),
            pltpu.VMEM((5, lt, SB, 128), f32),
            pltpu.VMEM((rows, lt, SB, 128), f32),
            pltpu.VMEM((rows, lt, SB, 128), f32),
            pltpu.VMEM((nblk, 5, SB, 128), f32),
            pltpu.VMEM((SB, 128), f32),
            pltpu.VMEM((nx, SB, 128), f32),
            pltpu.VMEM((na, SB, 128), f32),
            pltpu.VMEM((SB, 128), f32),
            dma((2, rows)), dma((2, rows)), dma((2, nblk)), dma((2, nblk)),
            dma((nx - 1,)), dma((nx - 1,)), dma((na - 1,)), dma((na - 1,)),
        ],
        compiler_params=pltpu.CompilerParams(
            dimension_semantics=("arbitrary",), collective_id=0, has_side_effects=True,
            vmem_limit_bytes=63 << 20),
        cost_estimate=pl.CostEstimate(
            flops=state.size * 90, bytes_accessed=state.size * 12, transcendentals=0),
        name="radial_part",
    )(state, start, state, state, sums)


def rows_kernel(cfg, *refs):
    r0, lt, nblk, share = cfg
    state, ahead, lo, hi, left, right, part = refs[:7]
    out = refs[-17]
    U, F, DF, DU, FF, SX, UZ, FZ, DFZ, DUZ, FFZ, SZ, TZ, AZ, LT, RT = refs[-16:]
    st = nblk * SB
    cells = lt * 128
    nz = cells // SB
    step = 2 * SB
    turns = cells // step
    per_turn = nblk // turns
    per_line = nz // nblk
    i = pl.program_id(0)
    lr = i + r0
    every = slice(None)
    sub = lax.broadcasted_iota(jnp.int32, (SB, 128), 0)

    line = lax.axis_index("ax")
    at_low = line == 0
    at_high = line == lax.axis_size("ax") - 1

    def block(b):
        return pl.ds(b * SB if isinstance(b, int) else pl.multiple_of(b * SB, SB), SB)

    def line_cells(u, b):
        rinv, p, cs = primitives(u)
        vel = u[3] * rinv
        f = fluxes(u, vel, p, 3)
        ds = block(b)
        for c in range(5):
            U[c, :, ds, :] = u[c]
            F[c, :, ds, :] = f[c]
        SX[:, ds, :] = jnp.abs(vel) + cs

    def line_end(ref, at_end, b, edge, to):
        u = []
        for c in range(5):
            inner = tiles(state, c, block(b))[:, edge:edge + 1]
            u.append(jnp.where(at_end, jnp.broadcast_to(inner, (lt, SB, 128)), tiles(ref, c, every)))
        line_cells(u, to)

    def line_block(b):
        line_cells([tiles(state, c, block(b)) for c in range(5)], b + 1)

    def turned_tile(src, t):
        c, l = t // lt, t % lt
        at = 128 * l
        if not isinstance(t, int):
            at = pl.multiple_of(at, 128)
        UZ[c, 0, pl.ds(at + SB, 128), :] = src[c, :, pl.ds(at, 128)].T

    def cycle_ends(row):
        for c in range(5):
            UZ[c, 0, pl.ds(0, SB), :] = pltpu.roll(LT[c, block(row), :], 5, 0)
            UZ[c, 0, pl.ds(SB + cells, SB), :] = pltpu.roll(RT[c, block(row), :], 5, 0)

    def cycle_cells(b):
        ds = block(b)
        u = [UZ[c, :, ds, :] for c in range(5)]
        rinv, p, cs = primitives(u)
        vel = u[2] * rinv
        f = fluxes(u, vel, p, 2)
        for c in range(5):
            FZ[c, :, ds, :] = f[c]
        SZ[:, ds, :] = jnp.abs(vel) + cs

    lines = ((F, DF), (U, DU))
    cycles = ((FZ, DFZ), (UZ, DUZ))

    def diff_block(pairs, b):
        o = b * SB if isinstance(b, int) else pl.multiple_of(b * SB, SB)
        for X, D in pairs:
            for c in range(5):
                D[c, :, pl.ds(o, SB), :] = X[c, :, pl.ds(o + 1, SB), :] - X[c, :, pl.ds(o, SB), :]

    def diff_last(pairs, b):
        for X, D in pairs:
            for c in range(5):
                x = X[c, :, block(b), :]
                D[c, :, block(b), :] = pltpu.roll(x, SB - 1, 1) - x

    def faces(F, DF, DU, S, c, base, n):
        df = [DF[c, :, pl.ds(base + k, n), :] for k in range(-2, 3)]
        du = [DU[c, :, pl.ds(base + k, n), :] for k in range(-2, 3)]
        a = jnp.maximum(S[:, pl.ds(base, n), :], S[:, pl.ds(base + 1, n), :])
        return face_flux12(df, du, a, F[c, :, pl.ds(base, n), :] + F[c, :, pl.ds(base + 1, n), :])

    def first_faces(F, DF, DU, S, FF):
        e = SB - 1
        for l in range(F.shape[1]):
            def pick(X, k):
                x = X[0, l, pl.ds(e + k, SB), :]
                for c in range(1, 5):
                    x = jnp.where(sub == c, X[c, l, pl.ds(e + k - c, SB), :], x)
                return x

            df = [pick(DF, k) for k in range(-2, 3)]
            du = [pick(DU, k) for k in range(-2, 3)]
            a = jnp.maximum(S[l, pl.ds(e, 1), :], S[l, pl.ds(e + 1, 1), :])
            f = face_flux12(df, du, a, pick(F, 0) + pick(F, 1))
            for c in range(5):
                FF[c, l, pl.ds(e, 1), :] = f[c:c + 1]

    gain = SECTION_GAIN * TIME_STEP
    radius = INNER_RADIUS + RADIAL_STEP * (lr.astype(jnp.float32) + 0.5)
    rr = 1.0 / jnp.full((1, 1, 128), radius, jnp.float32)
    k_cycle = (gain / 12.0 * NA / (2.0 * math.pi)) * rr
    k_line = gain / 12.0 / AXIAL_STEP

    @pl.when(i == 0)
    def _():
        for c in range(5):
            LT[c] = left[:, c].reshape(st, 128).T
            RT[c] = right[:, c].reshape(st, 128).T
        for t in range(5 * lt):
            turned_tile(state, t)
        cycle_ends(lr)

        def cells_loop(b, _):
            cycle_cells(b)
            return 0

        def diff_loop(b, _):
            diff_block(cycles, b)
            return 0

        lax.fori_loop(0, nz + 2, cells_loop, 0)
        lax.fori_loop(0, nz + 1, diff_loop, 0)
        diff_last(cycles, nz + 1)
        first_faces(FZ, DFZ, DUZ, SZ, FFZ)

    def cycle_turn(b, _):
        base = pl.multiple_of(b * step + SB, SB)
        for c in range(5):
            fa = faces(FZ, DFZ, DUZ, SZ, c, base, step)
            FFZ[c, :, pl.ds(base, step), :] = fa
            TZ[c, pl.ds(pl.multiple_of(b * step, step), step), :] = (
                k_cycle * (FFZ[c, :, pl.ds(base - 1, step), :] - fa))[0]
        for j in range(per_turn):
            diff_block(lines, jnp.maximum(per_turn * b - per_turn + j, 0))
        for j in range(per_turn):
            line_block(per_turn * b + j)
        turned_tile(ahead, jnp.minimum(b, 5 * lt - 1))
        return 0

    lax.fori_loop(0, turns, cycle_turn, 0)

    line_end(lo, at_low, 0, 0, 0)
    line_end(hi, at_high, nblk - 1, SB - 1, nblk + 1)
    diff_block(lines, 0)
    for b in range(nblk - per_turn, nblk + 1):
        diff_block(lines, b)
    diff_last(lines, nblk + 1)
    first_faces(F, DF, DU, SX, FF)
    for c in range(5):
        for l in range(lt):
            AZ[c, l] = TZ[c, pl.ds(128 * l, 128), :].T
    cycle_ends(jnp.minimum(lr + 1, r0 + pl.num_programs(0) - 1))

    def line_turn(b, _):
        hs = block(b)
        base = pl.multiple_of(b * SB + SB, SB)
        for c in range(5):
            fx = faces(F, DF, DU, SX, c, base, SB)
            FF[c, :, pl.ds(base, SB), :] = fx
            delta = k_line * (FF[c, :, pl.ds(base - 1, SB), :] - fx) + AZ[c, :, hs, :]
            for l in range(lt):
                ls = slice(128 * l, 128 * l + 128)
                value = part[c, hs, ls] + delta[l]
                if share:
                    at = b * SB
                    out[at // share, c, pl.ds(pl.multiple_of(at % share, SB), SB), ls] = value
                else:
                    out[c, hs, ls] = value
        for j in range(per_line):
            diff_block(cycles, jnp.maximum(per_line * b - per_line - 1 + j, 0))
        for j in range(per_line):
            cycle_cells(per_line * b + j)
        return 0

    lax.fori_loop(0, nblk, line_turn, 0)

    cycle_cells(nz)
    cycle_cells(nz + 1)
    for b in range(nz - per_line - 1, nz + 1):
        diff_block(cycles, b)
    diff_last(cycles, nz + 1)
    first_faces(FZ, DFZ, DUZ, SZ, FFZ)


def rk_rows(state, lo, hi, left, right, part, r0, r1, share=0, into=None):
    _, rows, stations, cells = state.shape
    lt = cells // 128
    nblk = stations // SB
    f32 = jnp.float32
    any_spec = pl.BlockSpec(memory_space=pl.ANY)
    row_spec = pl.BlockSpec((5, None, stations, cells), lambda i: (0, i + r0, 0, 0))
    end_spec = pl.BlockSpec((5, None, SB, cells), lambda i: (0, i + r0, 0, 0))
    pack_spec = pl.BlockSpec((nblk, 5, SB, 128), lambda i: (0, 0, 0, 0))
    ahead_spec = pl.BlockSpec(
        (5, None, stations, cells), lambda i: (0, jnp.minimum(i + r0 + 1, r1 - 1), 0, 0))
    in_specs = [row_spec, ahead_spec, end_spec, end_spec, pack_spec, pack_spec, row_spec]
    args = [state, state, lo, hi, left, right, part]
    alias = {}
    if share:
        groups = stations // share
        out_shape = jax.ShapeDtypeStruct((groups, 5, r1 - r0, share, cells), f32)
        out_spec = pl.BlockSpec((groups, 5, None, share, cells), lambda i: (0, 0, i, 0, 0))
    else:
        if into is not None:
            in_specs.append(any_spec)
            args.append(into)
            alias = {7: 0}
        out_shape, out_spec = jax.ShapeDtypeStruct(state.shape, f32), row_spec
    field = pltpu.VMEM((lt, stations + 2 * SB, 128), f32)
    group = pltpu.VMEM((5, lt, stations + 2 * SB, 128), f32)
    field_z = pltpu.VMEM((1, cells + 2 * SB, stations), f32)
    group_z = pltpu.VMEM((5, 1, cells + 2 * SB, stations), f32)
    return pl.pallas_call(
        functools.partial(rows_kernel, (r0, lt, nblk, share)),
        out_shape=out_shape,
        grid=(r1 - r0,),
        in_specs=in_specs,
        out_specs=out_spec,
        scratch_shapes=[group] * 5 + [field] + [group_z] * 5 + [
            field_z,
            pltpu.VMEM((5, cells, stations), f32),
            pltpu.VMEM((5, lt, stations, 128), f32),
            pltpu.VMEM((5, 128, stations), f32),
            pltpu.VMEM((5, 128, stations), f32),
        ],
        input_output_aliases=alias,
        compiler_params=pltpu.CompilerParams(
            dimension_semantics=("arbitrary",), vmem_limit_bytes=63 << 20),
        cost_estimate=pl.CostEstimate(
            flops=5 * (r1 - r0) * stations * cells * 180,
            bytes_accessed=5 * (r1 - r0) * stations * cells * 12, transcendentals=0),
        name="rk_rows_%d_%d" % (r0, r1),
    )(*args)


def place_kernel(final, whole, loads, out, gores):
    groups, _, share, cells = final.shape
    gores[...] = loads[0:1, 0:GORES].reshape(GORES)
    for g in range(groups):
        out[:, g * share:(g + 1) * share, :] = final[g]


def place_near(final, whole, loads):
    groups, _, _, share, cells = final.shape
    return pl.pallas_call(
        place_kernel,
        out_shape=(jax.ShapeDtypeStruct(whole.shape, jnp.float32),
                   jax.ShapeDtypeStruct((GORES,), jnp.float32)),
        grid=(NF,),
        in_specs=[pl.BlockSpec((groups, 5, None, share, cells), lambda i: (0, 0, i, 0, 0)),
                  pl.BlockSpec(memory_space=pl.ANY),
                  pl.BlockSpec((SB, 128), lambda i: (0, 0))],
        out_specs=(pl.BlockSpec((5, None, groups * share, cells), lambda i: (0, i, 0, 0)),
                   pl.BlockSpec((GORES,), lambda i: (0,))),
        input_output_aliases={1: 0},
        compiler_params=pltpu.CompilerParams(vmem_limit_bytes=63 << 20),
        name="place_near",
    )(final, whole, loads)


def mode_tables():
    n = np.arange(NA // 2)[:, None]
    tables = []
    for parity in (0, 1):
        k = np.arange(parity, NA // 4, 2)[None, :]
        angle = 2.0 * math.pi / NA * ((n * k) % NA)
        table = np.concatenate([np.cos(angle), np.sin(angle)], axis=1).astype(np.float32)
        high = table.astype(jnp.bfloat16)
        tables += [high, (table - high.astype(np.float32)).astype(jnp.bfloat16)]
    return tables


def split(x):
    high = x.astype(jnp.bfloat16)
    return high, (x - high.astype(jnp.float32)).astype(jnp.bfloat16)


def product(x, y, dims):
    x_high, x_low = x
    y_high, y_low = y

    def dot(a, b):
        return lax.dot_general(a, b, (dims, ((), ())), preferred_element_type=jnp.float32)

    return dot(x_high, y_high) + (dot(x_low, y_high) + dot(x_high, y_low))


def low_pass_kernel(cycles, cutoff, near_rows, even_high, even_low, odd_high, odd_low, final,
                    x, out, coef, tables, turned, come, go, fetch):
    pieces, _, _, share, cells = x.shape
    m = 5 * NF * share
    half = pieces // 2
    arrive = [pltpu.make_async_copy(cycles.at[p], x.at[p], come.at[p]) for p in range(pieces)]
    leave = [pltpu.make_async_copy(out.at[p], final.at[p], go.at[p]) for p in range(pieces)]
    source = (even_high, even_low, odd_high, odd_low)
    get = [
        [
            pltpu.make_async_copy(
                source[t].at[pl.ds(p * cells, cells), :], tables.at[t, pl.ds(p * cells, cells), :],
                fetch.at[p, t])
            for t in range(4)
        ]
        for p in range(half)
    ]
    for p in range(half):
        arrive[p].start()
        arrive[p + half].start()
        for cp in get[p]:
            cp.start()

    modes = tables.shape[2] // 2
    chosen = lax.broadcasted_iota(jnp.int32, cutoff.shape, 0) < near_rows[...]
    signed = jnp.where(chosen, cutoff[...], -cutoff[...]).astype(jnp.float32)
    turned[...] = jnp.concatenate([signed, signed], axis=0).T
    here = turned[pl.ds(pl.multiple_of(lax.axis_index("az") * share, SB), share), :]
    signs = jnp.concatenate([here[:, j:j + 1] for j in range(NF)] * 5, axis=0)
    limit = jnp.abs(signs).astype(jnp.int32)
    take = signs > 0.0

    for p in range(half):
        arrive[p].wait()
        arrive[p + half].wait()
        for cp in get[p]:
            cp.wait()
        x0 = x[p].reshape(m, cells)
        x1 = x[p + half].reshape(m, cells)
        at = slice(p * cells, (p + 1) * cells)
        for parity, part in enumerate((x0 + x1, x0 - x1)):
            rhs = (tables[2 * parity, at, :], tables[2 * parity + 1, at, :])
            value = product(split(part), rhs, ((1,), (0,)))
            coef[parity] = value if p == 0 else coef[parity] + value
    column = lax.broadcasted_iota(jnp.int32, (m, 2 * modes), 1)
    column = jnp.where(column < modes, column, column - modes)
    back = []
    for parity in range(2):
        k = 2 * column + parity
        weight = jnp.where(k == 0, 1.0 / NA, 2.0 / NA)
        gains = jnp.where(k < limit, weight, 0.0)
        back.append(split(coef[parity] * gains))
    for p in range(half):
        at = slice(p * cells, (p + 1) * cells)
        y0, y1 = (
            product(back[parity], (tables[2 * parity, at, :], tables[2 * parity + 1, at, :]), ((1,), (1,)))
            for parity in range(2)
        )
        for q, y in ((p, y0 + y1), (p + half, y0 - y1)):
            kept = jnp.where(take, y, x[q].reshape(m, cells))
            out[q] = kept.reshape(5, NF, share, cells)
            leave[q].start()
    for cp in leave:
        cp.wait()


def low_pass(cycles, cutoff, near_rows):
    pieces = cycles.shape[0]
    tables = [jnp.asarray(t) for t in mode_tables()]
    any_spec = pl.BlockSpec(memory_space=pl.ANY)
    vmem = pl.BlockSpec(memory_space=pltpu.VMEM)
    dma = pltpu.SemaphoreType.DMA
    return pl.pallas_call(
        low_pass_kernel,
        out_shape=jax.ShapeDtypeStruct(cycles.shape, jnp.float32),
        in_specs=[any_spec, vmem, vmem] + [any_spec] * 4,
        out_specs=any_spec,
        scratch_shapes=[
            pltpu.VMEM(cycles.shape, jnp.float32),
            pltpu.VMEM(cycles.shape, jnp.float32),
            pltpu.VMEM((2, 5 * NF * cycles.shape[3], NA // 4), jnp.float32),
            pltpu.VMEM((4, NA // 2, NA // 4), jnp.bfloat16),
            pltpu.VMEM((cutoff.shape[1], 2 * NF), jnp.float32),
            dma((pieces,)), dma((pieces,)), dma((pieces // 2, 4)),
        ],
        compiler_params=pltpu.CompilerParams(vmem_limit_bytes=63 << 20),
        name="low_pass",
    )(cycles, cutoff, near_rows[None], *tables)


def pressure_of(conserved):
    density = conserved[0]
    kinetic = (
        0.5
        * (conserved[1] * conserved[1] + conserved[2] * conserved[2] + conserved[3] * conserved[3])
        / density
    )
    return (HEAT_RATIO - 1.0) * (conserved[4] - kinetic)


def per_device(step_start, section_state, near_rows, cutoff, gore_map):
    _, rows, stations, cells = section_state.shape
    na, nx = lax.axis_size("az"), lax.axis_size("ax")
    line_index = lax.axis_index("ax")
    canopy = rows // 2
    jump = pressure_of(section_state[:, canopy - 1]) - pressure_of(section_state[:, canopy + 1])
    total = stations * nx
    station = line_index * stations + jnp.arange(stations, dtype=jnp.int32)
    ramp = 1.0 + 2.0 * station.astype(jnp.float32) / total
    weighted = jump * ramp[:, None] * (1.0 / math.sqrt(total * NA / GORES))
    gores = jnp.arange(GORES, dtype=jnp.int32)
    partial = jnp.sum(
        jnp.where(gore_map[None] == gores[:, None, None], weighted[None], 0.0), axis=(1, 2))
    part, left, right, lo, hi, loads = radial_part(section_state, step_start, partial, na, nx)

    rest = functools.partial(rk_rows, section_state, lo, hi, left, right, part)
    share = stations // na
    near = rest(0, NF, share=share)
    spread = lax.all_to_all(near, "az", 0, 0, tiled=True)
    middle = NF + (rows - NF) // 2
    whole = rest(NF, middle)
    spread, whole = lax.optimization_barrier((spread, whole))
    kept = low_pass(spread, cutoff, near_rows)
    kept, whole = lax.optimization_barrier((kept, whole))
    final = lax.all_to_all(kept, "az", 0, 0, tiled=True)
    whole = rest(middle, rows, into=whole)

    return tuple(place_near(final, whole, loads))


def solution(mesh):
    in_specs = (
        P(None, None, "ax", "az"),
        P(None, None, "ax", "az"),
        P("ax"),
        P(None, "ax"),
        P("ax", "az"),
    )
    out_specs = (P(None, None, "ax", "az"), P())
    return jax.shard_map(
        per_device, mesh=mesh, in_specs=in_specs, out_specs=out_specs, check_vma=False
    )
```

```python
import functools
import math

import jax
import jax.numpy as jnp
import numpy as np
from jax import lax
from jax.experimental import pallas as pl
from jax.experimental.pallas import tpu as pltpu
from jax.sharding import PartitionSpec as P

NA = 2048
NF = 4
GORES = 80

HEAT_RATIO = 1.4
WEIGHT_EPSILON = 1e-06
INNER_RADIUS = 24.0
RADIAL_STEP = 0.5
AXIAL_STEP = 0.5
TIME_STEP = 0.01
SECTION_KEEP = 1.0 / 3.0
SECTION_GAIN = 2.0 / 3.0

SB = 8
EPS = 3.0 * WEIGHT_EPSILON


def side(d1, d2, d3, d4):
    e1 = d2 - d1
    e2 = d3 - d2
    e3 = d4 - d3
    h2 = 0.75 * d2
    h3 = 0.75 * d3
    g2 = h2 * d2 + EPS
    g3 = h3 * d3 + EPS
    s1 = e1 * (e1 + h2) + g2
    s2 = e2 * (e2 + h2) + g2
    s3 = e3 * (e3 - h3) + g3
    t1 = s2 * pl.reciprocal(s1, approx=False)
    t3 = s2 * pl.reciprocal(s3, approx=False)
    w1 = t1 * t1
    w3 = 3.0 * (t3 * t3)
    num = (w1 + w1) * (e1 - e2) + w3 * (e2 - e3)
    return num * pl.reciprocal((w1 + 6.0) + w3, approx=False), e2


def face_flux12(df, du, a, fsum):
    au = [a * x for x in du]
    pm2, pm1, p0, p1 = (df[k] + au[k] for k in range(4))
    mm1, m0, m1, m2 = (df[k] - au[k] for k in range(1, 5))
    cp, ep = side(pm2, pm1, p0, p1)
    cm, em = side(m2, m1, m0, mm1)
    return 6.0 * fsum + ((cp - cm) - (ep - em))


def primitives(u):
    rinv = 1.0 / u[0]
    kin = 0.5 * (u[1] * u[1] + u[2] * u[2] + u[3] * u[3]) * rinv
    p = (HEAT_RATIO - 1.0) * (u[4] - kin)
    cs = jnp.sqrt(HEAT_RATIO * p * rinv)
    return rinv, p, cs


def fluxes(u, vel, p, normal):
    f = [u[normal], u[1] * vel, u[2] * vel, u[3] * vel, (u[4] + p) * vel]
    f[normal] = f[normal] + p
    return f


def tiles(ref, *ix):
    cells = ref.shape[-1]
    return jnp.stack([ref[(*ix, slice(128 * l, 128 * l + 128))] for l in range(cells // 128)])


def radial_kernel(rows, lt, na, nx, state, start, low_end, high_end, sums,
                  part, left, right, lo, hi, total,
                  DR, SR, RF, LF, S1, S2, pack, own, from_ax, from_az, line_sum,
                  end_send, end_recv, pack_send, pack_recv, ax_send, ax_recv, az_send, az_recv):
    i = pl.program_id(0)
    every = slice(None)
    me_a, me_x = lax.axis_index("az"), lax.axis_index("ax")
    nblk = pack.shape[0]
    per_step = rows // nblk
    assert per_step * nblk == rows
    MESH = pl.DeviceIdType.MESH

    def peer_a(d):
        return {"az": lax.rem(me_a + d, na)}

    def peer_x(d):
        return {"ax": lax.rem(me_x + d, nx)}

    def copy(src, dst, send, recv, peer):
        return pltpu.make_async_remote_copy(
            src_ref=src, dst_ref=dst, send_sem=send, recv_sem=recv,
            device_id=peer, device_id_type=MESH)

    def end_copies(r):
        return [
            copy(high_end.at[:, r], lo.at[:, r], end_send.at[0, r], end_recv.at[0, r], peer_x(1)),
            copy(low_end.at[:, r], hi.at[:, r], end_send.at[1, r], end_recv.at[1, r], peer_x(nx - 1)),
        ]

    def pack_copies(b):
        return [
            copy(pack.at[b], left.at[b], pack_send.at[0, b], pack_recv.at[0, b], peer_a(1)),
            copy(pack.at[b], right.at[b], pack_send.at[1, b], pack_recv.at[1, b], peer_a(na - 1)),
        ]

    def line_copies():
        return [
            copy(own, from_ax.at[me_x], ax_send.at[d], ax_recv.at[d], peer_x(d + 1))
            for d in range(nx - 1)
        ]

    def cycle_copies():
        return [
            copy(line_sum, from_az.at[me_a], az_send.at[d], az_recv.at[d], peer_a(d + 1))
            for d in range(na - 1)
        ]

    def ordered_sum(ref, count):
        value = ref[0]
        for d in range(1, count):
            value = value + ref[d]
        return value

    @pl.when(i == 0)
    def _():
        barrier = pltpu.get_barrier_semaphore()
        for d in range(1, na):
            pl.semaphore_signal(barrier, inc=1, device_id=peer_a(d), device_id_type=MESH)
        for d in range(1, nx):
            pl.semaphore_signal(barrier, inc=1, device_id=peer_x(d), device_id_type=MESH)
        own[...] = jnp.zeros((SB, 128), jnp.float32)
        own[0:1, 0:GORES] = sums[...].reshape(1, GORES)
        for e in (0, 1, 2, rows + 2, rows + 3, rows + 4):
            DR[:, :, e] = jnp.zeros((5, 2, lt, SB, 128), jnp.float32)

    @pl.when(i == 1)
    def _():
        pl.semaphore_wait(pltpu.get_barrier_semaphore(), na + nx - 2)
        for cp in line_copies():
            cp.start()

    @pl.when(i == nblk // 4)
    def _():
        for cp in line_copies():
            cp.wait()
        from_ax[me_x] = own[...]
        line_sum[...] = ordered_sum(from_ax, nx)
        for cp in cycle_copies():
            cp.start()

    lane = lax.broadcasted_iota(jnp.int32, (SB, 128), 1)
    near_side = lane < 64
    owner = lane // 8

    def cell(q):
        u = [tiles(state, c, q, every) for c in range(5)]
        rinv, p, cs = primitives(u)
        vel = u[1] * rinv
        swirl = u[2] * rinv
        S1[q] = u[2] * swirl + p
        S2[q] = u[1] * swirl
        return u, fluxes(u, vel, p, 1), jnp.abs(vel) + cs

    def edge(e, carry):
        u, f, s = carry[:5], carry[5:10], carry[10]
        un, fn, sn = cell(e - 2)
        for c in range(5):
            DR[c, 0, e] = fn[c] - f[c]
            DR[c, 1, e] = un[c] - u[c]
            RF[c, e] = fn[c] + f[c]
        SR[e] = jnp.maximum(s, sn)
        return (*un, *fn, sn)

    u, f, s = cell(0)
    for c in range(5):
        RF[c, 2] = f[c] + f[c]
    SR[2] = s
    last = lax.fori_loop(3, rows + 2, edge, (*u, *f, s))
    for c in range(5):
        RF[c, rows + 2] = last[5 + c] + last[5 + c]
    SR[rows + 2] = last[10]

    def face(c, e):
        df = [DR[c, 0, e + k] for k in range(-2, 3)]
        du = [DR[c, 1, e + k] for k in range(-2, 3)]
        return face_flux12(df, du, SR[e], RF[c, e])

    for c in range(5):
        value = None
        for q in range(rows):
            ends = jnp.where(near_side, state[c, q, :, 0:128], state[c, q, :, 128 * (lt - 1):128 * lt])
            ends = pltpu.roll(ends, (8 * q + 3) % 128, 1)
            value = ends if q == 0 else jnp.where(owner == q, ends, value)
        pack[i, c] = value
        LF[c] = face(c, 2)

    def send(b):
        for cp in pack_copies(b):
            cp.start()
        for j in range(per_step):
            for cp in end_copies(b * per_step + j):
                cp.start()

    @pl.when(i > 0)
    def _():
        send(i - 1)

    @pl.when(i == nblk - 1)
    def _():
        send(i)

    gain = SECTION_GAIN * TIME_STEP

    def one_row(r, _):
        row = r.astype(jnp.float32)
        radius = INNER_RADIUS + RADIAL_STEP * (row + 0.5)
        rr = 1.0 / jnp.full((1, 1, 128), radius, jnp.float32)
        k_low = (gain / 12.0 / RADIAL_STEP) * (INNER_RADIUS + RADIAL_STEP * row) * rr
        k_up = (gain / 12.0 / RADIAL_STEP) * (INNER_RADIUS + RADIAL_STEP * (row + 1.0)) * rr
        k_src = gain * rr
        for c in range(5):
            up = face(c, r + 3)
            value = k_low * LF[c] - k_up * up
            LF[c] = up
            value = value + (SECTION_KEEP * tiles(start, c, r, every) + SECTION_GAIN * tiles(state, c, r, every))
            if c == 1:
                value = value + k_src * S1[r]
            if c == 2:
                value = value - k_src * S2[r]
            for l in range(lt):
                part[c, r, :, 128 * l:128 * l + 128] = value[l]
        return 0

    lax.fori_loop(0, rows, one_row, 0)

    @pl.when(i == nblk - 1)
    def _():
        for cp in cycle_copies():
            cp.wait()
        from_az[me_a] = line_sum[...]
        total[...] = ordered_sum(from_az, na)

        def finish(b, _):
            for cp in pack_copies(b):
                cp.wait()
            for j in range(per_step):
                for cp in end_copies(b * per_step + j):
                    cp.wait()
            return 0

        lax.fori_loop(0, nblk, finish, 0)


def radial_part(state, start, sums, na, nx):
    _, rows, stations, cells = state.shape
    lt = cells // 128
    nblk = stations // SB
    f32 = jnp.float32
    spec = pl.BlockSpec((5, rows, SB, cells), lambda i: (0, 0, i, 0))
    low_spec = pl.BlockSpec((5, rows, SB, cells), lambda i: (0, 0, 0, 0))
    high_spec = pl.BlockSpec((5, rows, SB, cells), lambda i: (0, 0, nblk - 1, 0))
    small = pl.BlockSpec((SB, 128), lambda i: (0, 0))
    any_spec = pl.BlockSpec(memory_space=pl.ANY)
    side = jax.ShapeDtypeStruct((nblk, 5, SB, 128), f32)
    end = jax.ShapeDtypeStruct((5, rows, SB, cells), f32)
    dma = pltpu.SemaphoreType.DMA
    return pl.pallas_call(
        functools.partial(radial_kernel, rows, lt, na, nx),
        out_shape=(jax.ShapeDtypeStruct(state.shape, f32), side, side, end, end,
                   jax.ShapeDtypeStruct((SB, 128), f32)),
        grid=(nblk,),
        in_specs=[spec, spec, low_spec, high_spec, pl.BlockSpec((GORES,), lambda i: (0,))],
        out_specs=(spec,) + (any_spec,) * 4 + (small,),
        scratch_shapes=[
            pltpu.VMEM((5, 2, rows + 5, lt, SB, 128), f32),
            pltpu.VMEM((rows + 5, lt, SB, 128), f32),
            pltpu.VMEM((5, rows + 5, lt, SB, 128), f32),
            pltpu.VMEM((5, lt, SB, 128), f32),
            pltpu.VMEM((rows, lt, SB, 128), f32),
            pltpu.VMEM((rows, lt, SB, 128), f32),
            pltpu.VMEM((nblk, 5, SB, 128), f32),
            pltpu.VMEM((SB, 128), f32),
            pltpu.VMEM((nx, SB, 128), f32),
            pltpu.VMEM((na, SB, 128), f32),
            pltpu.VMEM((SB, 128), f32),
            dma((2, rows)), dma((2, rows)), dma((2, nblk)), dma((2, nblk)),
            dma((nx - 1,)), dma((nx - 1,)), dma((na - 1,)), dma((na - 1,)),
        ],
        compiler_params=pltpu.CompilerParams(
            dimension_semantics=("arbitrary",), collective_id=0, has_side_effects=True,
            vmem_limit_bytes=63 << 20),
        cost_estimate=pl.CostEstimate(
            flops=state.size * 90, bytes_accessed=state.size * 12, transcendentals=0),
        name="radial_part",
    )(state, start, state, state, sums)


def row_step(i, r0, count, lt, nblk, blocks, out, scratch):
    state, ahead, lo, hi, left, right, part = blocks
    U, F, DF, DU, FF, SX, UZ, FZ, DFZ, DUZ, FFZ, SZ, TZ, AZ, LT, RT = scratch
    st = nblk * SB
    cells = lt * 128
    nz = cells // SB
    step = 2 * SB
    turns = cells // step
    per_turn = nblk // turns
    per_line = nz // nblk
    lr = i + r0
    every = slice(None)
    sub = lax.broadcasted_iota(jnp.int32, (SB, 128), 0)

    line = lax.axis_index("ax")
    at_low = line == 0
    at_high = line == lax.axis_size("ax") - 1

    def block(b):
        return pl.ds(b * SB if isinstance(b, int) else pl.multiple_of(b * SB, SB), SB)

    def line_cells(u, b):
        rinv, p, cs = primitives(u)
        vel = u[3] * rinv
        f = fluxes(u, vel, p, 3)
        ds = block(b)
        for c in range(5):
            U[c, :, ds, :] = u[c]
            F[c, :, ds, :] = f[c]
        SX[:, ds, :] = jnp.abs(vel) + cs

    def line_end(ref, at_end, b, edge, to):
        u = []
        for c in range(5):
            inner = tiles(state, c, block(b))[:, edge:edge + 1]
            u.append(jnp.where(at_end, jnp.broadcast_to(inner, (lt, SB, 128)), tiles(ref, c, every)))
        line_cells(u, to)

    def line_block(b):
        line_cells([tiles(state, c, block(b)) for c in range(5)], b + 1)

    def turned_tile(src, t):
        c, l = t // lt, t % lt
        at = 128 * l
        if not isinstance(t, int):
            at = pl.multiple_of(at, 128)
        UZ[c, 0, pl.ds(at + SB, 128), :] = src[c, :, pl.ds(at, 128)].T

    def cycle_ends(row):
        for c in range(5):
            UZ[c, 0, pl.ds(0, SB), :] = pltpu.roll(LT[c, block(row), :], 5, 0)
            UZ[c, 0, pl.ds(SB + cells, SB), :] = pltpu.roll(RT[c, block(row), :], 5, 0)

    def cycle_cells(b):
        ds = block(b)
        u = [UZ[c, :, ds, :] for c in range(5)]
        rinv, p, cs = primitives(u)
        vel = u[2] * rinv
        f = fluxes(u, vel, p, 2)
        for c in range(5):
            FZ[c, :, ds, :] = f[c]
        SZ[:, ds, :] = jnp.abs(vel) + cs

    lines = ((F, DF), (U, DU))
    cycles = ((FZ, DFZ), (UZ, DUZ))

    def diff_block(pairs, b):
        o = b * SB if isinstance(b, int) else pl.multiple_of(b * SB, SB)
        for X, D in pairs:
            for c in range(5):
                D[c, :, pl.ds(o, SB), :] = X[c, :, pl.ds(o + 1, SB), :] - X[c, :, pl.ds(o, SB), :]

    def diff_last(pairs, b):
        for X, D in pairs:
            for c in range(5):
                x = X[c, :, block(b), :]
                D[c, :, block(b), :] = pltpu.roll(x, SB - 1, 1) - x

    def faces(F, DF, DU, S, c, base, n):
        df = [DF[c, :, pl.ds(base + k, n), :] for k in range(-2, 3)]
        du = [DU[c, :, pl.ds(base + k, n), :] for k in range(-2, 3)]
        a = jnp.maximum(S[:, pl.ds(base, n), :], S[:, pl.ds(base + 1, n), :])
        return face_flux12(df, du, a, F[c, :, pl.ds(base, n), :] + F[c, :, pl.ds(base + 1, n), :])

    def first_faces(F, DF, DU, S, FF):
        e = SB - 1
        for l in range(F.shape[1]):
            def pick(X, k):
                x = X[0, l, pl.ds(e + k, SB), :]
                for c in range(1, 5):
                    x = jnp.where(sub == c, X[c, l, pl.ds(e + k - c, SB), :], x)
                return x

            df = [pick(DF, k) for k in range(-2, 3)]
            du = [pick(DU, k) for k in range(-2, 3)]
            a = jnp.maximum(S[l, pl.ds(e, 1), :], S[l, pl.ds(e + 1, 1), :])
            f = face_flux12(df, du, a, pick(F, 0) + pick(F, 1))
            for c in range(5):
                FF[c, l, pl.ds(e, 1), :] = f[c:c + 1]

    gain = SECTION_GAIN * TIME_STEP
    radius = INNER_RADIUS + RADIAL_STEP * (lr.astype(jnp.float32) + 0.5)
    rr = 1.0 / jnp.full((1, 1, 128), radius, jnp.float32)
    k_cycle = (gain / 12.0 * NA / (2.0 * math.pi)) * rr
    k_line = gain / 12.0 / AXIAL_STEP

    @pl.when(i == 0)
    def _():
        for c in range(5):
            LT[c] = left[:, c].reshape(st, 128).T
            RT[c] = right[:, c].reshape(st, 128).T
        for t in range(5 * lt):
            turned_tile(state, t)
        cycle_ends(lr)

        def cells_loop(b, _):
            cycle_cells(b)
            return 0

        def diff_loop(b, _):
            diff_block(cycles, b)
            return 0

        lax.fori_loop(0, nz + 2, cells_loop, 0)
        lax.fori_loop(0, nz + 1, diff_loop, 0)
        diff_last(cycles, nz + 1)
        first_faces(FZ, DFZ, DUZ, SZ, FFZ)

    def cycle_turn(b, _):
        base = pl.multiple_of(b * step + SB, SB)
        for c in range(5):
            fa = faces(FZ, DFZ, DUZ, SZ, c, base, step)
            FFZ[c, :, pl.ds(base, step), :] = fa
            TZ[c, pl.ds(pl.multiple_of(b * step, step), step), :] = (
                k_cycle * (FFZ[c, :, pl.ds(base - 1, step), :] - fa))[0]
        for j in range(per_turn):
            diff_block(lines, jnp.maximum(per_turn * b - per_turn + j, 0))
        for j in range(per_turn):
            line_block(per_turn * b + j)
        turned_tile(ahead, jnp.minimum(b, 5 * lt - 1))
        return 0

    lax.fori_loop(0, turns, cycle_turn, 0)

    line_end(lo, at_low, 0, 0, 0)
    line_end(hi, at_high, nblk - 1, SB - 1, nblk + 1)
    diff_block(lines, 0)
    for b in range(nblk - per_turn, nblk + 1):
        diff_block(lines, b)
    diff_last(lines, nblk + 1)
    first_faces(F, DF, DU, SX, FF)
    for c in range(5):
        for l in range(lt):
            AZ[c, l] = TZ[c, pl.ds(128 * l, 128), :].T
    cycle_ends(r0 + (i + 1) % count)

    def line_turn(b, _):
        hs = block(b)
        base = pl.multiple_of(b * SB + SB, SB)
        for c in range(5):
            fx = faces(F, DF, DU, SX, c, base, SB)
            FF[c, :, pl.ds(base, SB), :] = fx
            delta = k_line * (FF[c, :, pl.ds(base - 1, SB), :] - fx) + AZ[c, :, hs, :]
            for l in range(lt):
                ls = slice(128 * l, 128 * l + 128)
                value = part[c, hs, ls] + delta[l]
                out[c, hs, ls] = value
        for j in range(per_line):
            diff_block(cycles, jnp.maximum(per_line * b - per_line - 1 + j, 0))
        for j in range(per_line):
            cycle_cells(per_line * b + j)
        return 0

    lax.fori_loop(0, nblk, line_turn, 0)

    cycle_cells(nz)
    cycle_cells(nz + 1)
    for b in range(nz - per_line - 1, nz + 1):
        diff_block(cycles, b)
    diff_last(cycles, nz + 1)
    first_faces(FZ, DFZ, DUZ, SZ, FFZ)


def send_kernel(count, middle, lt, nblk, na, *refs):
    blocks, (cutoff, near_rows), source = refs[:7], refs[7:9], refs[9:13]
    out, final = refs[13:15]
    scratch = refs[15:31]
    (near, spread, kept, coef, tables, turned,
     near_send, near_recv, near_own, kept_send, kept_recv, fetch) = refs[31:]
    share = spread.shape[3]
    i = pl.program_id(0)
    me = lax.axis_index("az")
    MESH = pl.DeviceIdType.MESH

    def peer(d):
        return lax.rem(me + d, na)

    def remote(src, dst, send, recv, d):
        return pltpu.make_async_remote_copy(
            src_ref=src, dst_ref=dst, send_sem=send, recv_sem=recv,
            device_id={"az": peer(d)}, device_id_type=MESH)

    def stations_of(g):
        return pl.ds(pl.multiple_of(g * share, SB), share)

    def near_copies(j):
        return [
            remote(near.at[j, :, stations_of(peer(d)), :], spread.at[me, :, j],
                   near_send.at[d - 1, j], near_recv.at[d - 1, j], d)
            for d in range(1, na)
        ] + [pltpu.make_async_copy(near.at[j, :, stations_of(me), :], spread.at[me, :, j], near_own.at[j])]

    def kept_copies():
        return [
            remote(kept.at[peer(d)], final.at[me], kept_send.at[d - 1], kept_recv.at[d - 1], d)
            for d in range(1, na)
        ] + [pltpu.make_async_copy(kept.at[me], final.at[me], near_own.at[NF])]

    def table_copies():
        return [pltpu.make_async_copy(source[t], tables.at[t], fetch.at[t]) for t in range(4)]

    @pl.when(i == 0)
    def _():
        barrier = pltpu.get_barrier_semaphore()
        for d in range(1, na):
            pl.semaphore_signal(barrier, inc=1, device_id={"az": peer(d)}, device_id_type=MESH)
        for cp in table_copies():
            cp.start()

    @pl.when(i == 1)
    def _():
        pl.semaphore_wait(pltpu.get_barrier_semaphore(), na - 1)

    @pl.when((i >= 1) & (i <= NF))
    def _():
        for cp in near_copies(i - 1):
            cp.start()

    @pl.when(i == middle)
    def _():
        for cp in table_copies():
            cp.wait()
        for j in range(NF):
            for cp in near_copies(j):
                cp.wait()
        low_pass(spread, kept, coef, tables, turned, cutoff, near_rows)
        for cp in kept_copies():
            cp.start()

    row_step(i, 0, count, lt, nblk, blocks, out, scratch)

    @pl.when(i < NF)
    def _():
        for c in range(5):
            near[i, c] = out[c]

    @pl.when(i == count - 1)
    def _():
        for cp in kept_copies():
            cp.wait()


def join_kernel(r0, count, lt, nblk, na, *refs):
    blocks, (whole, final, loads) = refs[:7], refs[7:10]
    result, gores = refs[10:12]
    scratch = refs[12:28]
    row_out, stage, stage_near, row_sem, come, go, come_near, go_near = refs[28:]
    share = stage_near.shape[3]
    i = pl.program_id(0)

    def in_copies():
        return [pltpu.make_async_copy(whole.at[:, r], stage.at[r - NF], come.at[r - NF])
                for r in range(NF, r0)] + [
            pltpu.make_async_copy(final.at[g], stage_near.at[g], come_near.at[g]) for g in range(na)]

    def out_copies():
        return [pltpu.make_async_copy(stage.at[r - NF], result.at[:, r], go.at[r - NF])
                for r in range(NF, r0)] + [
            pltpu.make_async_copy(
                stage_near.at[g], result.at[:, pl.ds(0, NF), pl.ds(g * share, share), :], go_near.at[g])
            for g in range(na)]

    def row_copy(j):
        return pltpu.make_async_copy(row_out.at[j], result.at[:, r0 + j], row_sem.at[j])

    @pl.when(i == 0)
    def _():
        gores[...] = loads[0:1, 0:GORES].reshape(GORES)
        for cp in in_copies():
            cp.start()

    @pl.when(i == 1)
    def _():
        for cp in in_copies():
            cp.wait()
        for cp in out_copies():
            cp.start()

    row_step(i, r0, count, lt, nblk, blocks, row_out.at[i], scratch)
    row_copy(i).start()

    @pl.when(i == count - 1)
    def _():
        for cp in out_copies():
            cp.wait()
        for j in range(count):
            row_copy(j).wait()


def row_call(kernel, name, r0, count, args, extra, extra_specs, out_shape, out_specs, more, **params):
    state = args[0]
    _, rows, stations, cells = state.shape
    lt = cells // 128
    nblk = stations // SB
    f32 = jnp.float32
    row_spec = pl.BlockSpec((5, None, stations, cells), lambda i: (0, r0 + i, 0, 0))
    ahead_spec = pl.BlockSpec((5, None, stations, cells), lambda i: (0, r0 + (i + 1) % count, 0, 0))
    end_spec = pl.BlockSpec((5, None, SB, cells), lambda i: (0, r0 + i, 0, 0))
    pack_spec = pl.BlockSpec((nblk, 5, SB, 128), lambda i: (0, 0, 0, 0))
    field = pltpu.VMEM((lt, stations + 2 * SB, 128), f32)
    group = pltpu.VMEM((5, lt, stations + 2 * SB, 128), f32)
    field_z = pltpu.VMEM((1, cells + 2 * SB, stations), f32)
    group_z = pltpu.VMEM((5, 1, cells + 2 * SB, stations), f32)
    return pl.pallas_call(
        kernel,
        out_shape=out_shape,
        grid=(count,),
        in_specs=[row_spec, ahead_spec, end_spec, end_spec, pack_spec, pack_spec, row_spec] + extra_specs,
        out_specs=out_specs(row_spec),
        scratch_shapes=[group] * 5 + [field] + [group_z] * 5 + [
            field_z,
            pltpu.VMEM((5, cells, stations), f32),
            pltpu.VMEM((5, lt, stations, 128), f32),
            pltpu.VMEM((5, 128, stations), f32),
            pltpu.VMEM((5, 128, stations), f32),
        ] + more,
        compiler_params=pltpu.CompilerParams(
            dimension_semantics=("arbitrary",), vmem_limit_bytes=63 << 20, **params),
        name=name,
    )(state, *args, *extra)


def rk_rows(state, lo, hi, left, right, part, cutoff, near_rows, loads, na):
    _, rows, stations, cells = state.shape
    lt = cells // 128
    nblk = stations // SB
    share = stations // na
    f32 = jnp.float32
    count = rows - 2
    middle = NF + 2 * (count - NF) // 5
    args = [state, lo, hi, left, right, part]
    any_spec = pl.BlockSpec(memory_space=pl.ANY)
    shape = (na, 5, NF, share, cells)
    pieces = pltpu.VMEM(shape, f32)
    whole_shape = jax.ShapeDtypeStruct(state.shape, f32)
    dma = pltpu.SemaphoreType.DMA
    whole, final = row_call(
        functools.partial(send_kernel, count, middle, lt, nblk, na), "rows_send", 0, count, args,
        [cutoff, near_rows[None], *(jnp.asarray(t) for t in mode_tables())],
        [pl.BlockSpec(cutoff.shape, lambda i: (0, 0)), pl.BlockSpec((1, stations), lambda i: (0, 0))]
        + [any_spec] * 4,
        (whole_shape, jax.ShapeDtypeStruct(shape, f32)),
        lambda row_spec: (row_spec, any_spec),
        [
            pltpu.VMEM((NF, 5, stations, cells), f32),
            pieces, pieces,
            pltpu.VMEM((2, 5 * NF * share, NA // 4), f32),
            pltpu.VMEM((4, NA // 2, NA // 4), jnp.bfloat16),
            pltpu.VMEM((stations, 2 * NF), f32),
            dma((na - 1, NF)), dma((na - 1, NF)), dma((NF + 1,)),
            dma((na - 1,)), dma((na - 1,)), dma((4,)),
        ],
        collective_id=1, has_side_effects=True)
    return row_call(
        functools.partial(join_kernel, count, rows - count, lt, nblk, na), "rows_join",
        count, rows - count, args,
        [whole, final, loads],
        [any_spec, any_spec, pl.BlockSpec((SB, 128), lambda i: (0, 0))],
        (whole_shape, jax.ShapeDtypeStruct((GORES,), f32)),
        lambda row_spec: (any_spec, pl.BlockSpec((GORES,), lambda i: (0,))),
        [
            pltpu.VMEM((rows - count, 5, stations, cells), f32),
            pltpu.VMEM((count - NF, 5, stations, cells), f32),
            pieces,
            dma((rows - count,)), dma((count - NF,)), dma((count - NF,)), dma((na,)), dma((na,)),
        ])


def mode_tables():
    n = np.arange(NA // 2)[:, None]
    tables = []
    for parity in (0, 1):
        k = np.arange(parity, NA // 4, 2)[None, :]
        angle = 2.0 * math.pi / NA * ((n * k) % NA)
        table = np.concatenate([np.cos(angle), np.sin(angle)], axis=1).astype(np.float32)
        high = table.astype(jnp.bfloat16)
        tables += [high, (table - high.astype(np.float32)).astype(jnp.bfloat16)]
    return tables


def split(x):
    high = x.astype(jnp.bfloat16)
    return high, (x - high.astype(jnp.float32)).astype(jnp.bfloat16)


def product(x, y, dims):
    x_high, x_low = x
    y_high, y_low = y

    def dot(a, b):
        return lax.dot_general(a, b, (dims, ((), ())), preferred_element_type=jnp.float32)

    return dot(x_high, y_high) + (dot(x_low, y_high) + dot(x_high, y_low))


def low_pass(x, out, coef, tables, turned, cutoff, near_rows):
    pieces, _, _, share, cells = x.shape
    m = 5 * NF * share
    half = pieces // 2
    modes = tables.shape[2] // 2
    chosen = lax.broadcasted_iota(jnp.int32, cutoff.shape, 0) < near_rows[...]
    signed = jnp.where(chosen, cutoff[...], -cutoff[...]).astype(jnp.float32)
    turned[...] = jnp.concatenate([signed, signed], axis=0).T
    here = turned[pl.ds(pl.multiple_of(lax.axis_index("az") * share, SB), share), :]
    signs = jnp.concatenate([here[:, j:j + 1] for j in range(NF)] * 5, axis=0)
    limit = jnp.abs(signs).astype(jnp.int32)
    take = signs > 0.0

    for p in range(half):
        x0 = x[p].reshape(m, cells)
        x1 = x[p + half].reshape(m, cells)
        at = slice(p * cells, (p + 1) * cells)
        for parity, part in enumerate((x0 + x1, x0 - x1)):
            rhs = (tables[2 * parity, at, :], tables[2 * parity + 1, at, :])
            value = product(split(part), rhs, ((1,), (0,)))
            coef[parity] = value if p == 0 else coef[parity] + value
    column = lax.broadcasted_iota(jnp.int32, (m, 2 * modes), 1)
    column = jnp.where(column < modes, column, column - modes)
    back = []
    for parity in range(2):
        k = 2 * column + parity
        weight = jnp.where(k == 0, 1.0 / NA, 2.0 / NA)
        gains = jnp.where(k < limit, weight, 0.0)
        back.append(split(coef[parity] * gains))
    for p in range(half):
        at = slice(p * cells, (p + 1) * cells)
        y0, y1 = (
            product(back[parity], (tables[2 * parity, at, :], tables[2 * parity + 1, at, :]), ((1,), (1,)))
            for parity in range(2)
        )
        for q, y in ((p, y0 + y1), (p + half, y0 - y1)):
            kept = jnp.where(take, y, x[q].reshape(m, cells))
            out[q] = kept.reshape(5, NF, share, cells)


def pressure_of(conserved):
    density = conserved[0]
    kinetic = (
        0.5
        * (conserved[1] * conserved[1] + conserved[2] * conserved[2] + conserved[3] * conserved[3])
        / density
    )
    return (HEAT_RATIO - 1.0) * (conserved[4] - kinetic)


def per_device(step_start, section_state, near_rows, cutoff, gore_map):
    _, rows, stations, cells = section_state.shape
    na, nx = lax.axis_size("az"), lax.axis_size("ax")
    line_index = lax.axis_index("ax")
    canopy = rows // 2
    jump = pressure_of(section_state[:, canopy - 1]) - pressure_of(section_state[:, canopy + 1])
    total = stations * nx
    station = line_index * stations + jnp.arange(stations, dtype=jnp.int32)
    ramp = 1.0 + 2.0 * station.astype(jnp.float32) / total
    weighted = jump * ramp[:, None] * (1.0 / math.sqrt(total * NA / GORES))
    gores = jnp.arange(GORES, dtype=jnp.int32)
    partial = jnp.sum(
        jnp.where(gore_map[None] == gores[:, None, None], weighted[None], 0.0), axis=(1, 2))
    part, left, right, lo, hi, loads = radial_part(section_state, step_start, partial, na, nx)

    return tuple(rk_rows(
        section_state, lo, hi, left, right, part, cutoff, near_rows, loads, na))


def solution(mesh):
    in_specs = (
        P(None, None, "ax", "az"),
        P(None, None, "ax", "az"),
        P("ax"),
        P(None, "ax"),
        P("ax", "az"),
    )
    out_specs = (P(None, None, "ax", "az"), P())
    return jax.shard_map(
        per_device, mesh=mesh, in_specs=in_specs, out_specs=out_specs, check_vma=False
    )
```

```python
import functools
import math

import jax
import jax.numpy as jnp
import numpy as np
from jax import lax
from jax.experimental import pallas as pl
from jax.experimental.pallas import tpu as pltpu
from jax.sharding import PartitionSpec as P

NA = 2048
NF = 4
GORES = 80

HEAT_RATIO = 1.4
WEIGHT_EPSILON = 1e-06
INNER_RADIUS = 24.0
RADIAL_STEP = 0.5
AXIAL_STEP = 0.5
TIME_STEP = 0.01
SECTION_KEEP = 1.0 / 3.0
SECTION_GAIN = 2.0 / 3.0

SB = 8
BEGIN = 3
EPS = 3.0 * WEIGHT_EPSILON


def side(d1, d2, d3, d4):
    e1 = d2 - d1
    e2 = d3 - d2
    e3 = d4 - d3
    h2 = 0.75 * d2
    h3 = 0.75 * d3
    g2 = h2 * d2 + EPS
    g3 = h3 * d3 + EPS
    s1 = e1 * (e1 + h2) + g2
    s2 = e2 * (e2 + h2) + g2
    s3 = e3 * (e3 - h3) + g3
    t1 = s2 * pl.reciprocal(s1, approx=False)
    t3 = s2 * pl.reciprocal(s3, approx=False)
    w1 = t1 * t1
    w3 = 3.0 * (t3 * t3)
    num = (w1 + w1) * (e1 - e2) + w3 * (e2 - e3)
    return num * pl.reciprocal((w1 + 6.0) + w3, approx=False), e2


def face_flux12(df, du, a, fsum):
    au = [a * x for x in du]
    pm2, pm1, p0, p1 = (df[k] + au[k] for k in range(4))
    mm1, m0, m1, m2 = (df[k] - au[k] for k in range(1, 5))
    cp, ep = side(pm2, pm1, p0, p1)
    cm, em = side(m2, m1, m0, mm1)
    return 6.0 * fsum + ((cp - cm) - (ep - em))


def primitives(u):
    rinv = 1.0 / u[0]
    kin = 0.5 * (u[1] * u[1] + u[2] * u[2] + u[3] * u[3]) * rinv
    p = (HEAT_RATIO - 1.0) * (u[4] - kin)
    cs = jnp.sqrt(HEAT_RATIO * p * rinv)
    return rinv, p, cs


def fluxes(u, vel, p, normal):
    f = [u[normal], u[1] * vel, u[2] * vel, u[3] * vel, (u[4] + p) * vel]
    f[normal] = f[normal] + p
    return f


def tiles(ref, *ix):
    cells = ref.shape[-1]
    return jnp.stack([ref[(*ix, slice(128 * l, 128 * l + 128))] for l in range(cells // 128)])


def radial_kernel(rows, lt, na, nx, state, start, head, tail, low_end, high_end, sums,
                  part, left, right, lo, hi, total,
                  DR, SR, RF, LF, S1, S2, pack, own, from_ax, from_az, line_sum,
                  end_send, end_recv, pack_send, pack_recv, ax_send, ax_recv, az_send, az_recv):
    i = pl.program_id(0)
    every = slice(None)
    me_a, me_x = lax.axis_index("az"), lax.axis_index("ax")
    turns = pack.shape[0]
    nblk = 2 * turns
    per_turn = rows // turns
    assert per_turn * turns == rows
    MESH = pl.DeviceIdType.MESH

    def peer_a(d):
        return {"az": lax.rem(me_a + d, na)}

    def peer_x(d):
        return {"ax": lax.rem(me_x + d, nx)}

    def copy(src, dst, send, recv, peer):
        return pltpu.make_async_remote_copy(
            src_ref=src, dst_ref=dst, send_sem=send, recv_sem=recv,
            device_id=peer, device_id_type=MESH)

    def end_copies(r):
        return [
            copy(high_end.at[:, r], lo.at[:, r], end_send.at[0, r], end_recv.at[0, r], peer_x(1)),
            copy(low_end.at[:, r], hi.at[:, r], end_send.at[1, r], end_recv.at[1, r], peer_x(nx - 1)),
        ]

    def pack_copies(b):
        return [
            copy(pack.at[b], left.at[b], pack_send.at[0, b], pack_recv.at[0, b], peer_a(1)),
            copy(pack.at[b], right.at[b], pack_send.at[1, b], pack_recv.at[1, b], peer_a(na - 1)),
        ]

    def line_copies():
        return [
            copy(own, from_ax.at[me_x], ax_send.at[d], ax_recv.at[d], peer_x(d + 1))
            for d in range(nx - 1)
        ]

    def cycle_copies():
        return [
            copy(line_sum, from_az.at[me_a], az_send.at[d], az_recv.at[d], peer_a(d + 1))
            for d in range(na - 1)
        ]

    def ordered_sum(ref, count):
        value = ref[0]
        for d in range(1, count):
            value = value + ref[d]
        return value

    @pl.when(i == 0)
    def _():
        barrier = pltpu.get_barrier_semaphore()
        for d in range(1, na):
            pl.semaphore_signal(barrier, inc=1, device_id=peer_a(d), device_id_type=MESH)
        for d in range(1, nx):
            pl.semaphore_signal(barrier, inc=1, device_id=peer_x(d), device_id_type=MESH)
        own[...] = jnp.zeros((SB, 128), jnp.float32)
        own[0:1, 0:GORES] = sums[...].reshape(1, GORES)
        for e in (0, 1, 2, rows + 2, rows + 3, rows + 4):
            DR[:, :, e] = jnp.zeros((5, 2, lt, SB, 128), jnp.float32)

    lane = lax.broadcasted_iota(jnp.int32, (2 * SB, 128), 1)
    near_side = lane < 64
    owner = lane // 8

    @pl.when(i < turns)
    def _():
        for c in range(5):
            value = None
            for q in range(rows):
                ends = pltpu.roll(jnp.where(near_side, head[c, q], tail[c, q]), (8 * q + 3) % 128, 1)
                value = ends if q == 0 else jnp.where(owner == q, ends, value)
            pack[i, c] = value

    @pl.when(i == BEGIN)
    def _():
        pl.semaphore_wait(pltpu.get_barrier_semaphore(), na + nx - 2)
        for cp in line_copies():
            cp.start()

    @pl.when((i >= BEGIN) & (i < BEGIN + turns))
    def _():
        b = i - BEGIN
        for cp in pack_copies(b):
            cp.start()
        for j in range(per_turn):
            for cp in end_copies(b * per_turn + j):
                cp.start()

    @pl.when(i == BEGIN + nblk // 4)
    def _():
        for cp in line_copies():
            cp.wait()
        from_ax[me_x] = own[...]
        line_sum[...] = ordered_sum(from_ax, nx)
        for cp in cycle_copies():
            cp.start()

    def cell(q):
        u = [tiles(state, c, q, every) for c in range(5)]
        rinv, p, cs = primitives(u)
        vel = u[1] * rinv
        swirl = u[2] * rinv
        S1[q] = u[2] * swirl + p
        S2[q] = u[1] * swirl
        return u, fluxes(u, vel, p, 1), jnp.abs(vel) + cs

    def edge(e, carry):
        u, f, s = carry[:5], carry[5:10], carry[10]
        un, fn, sn = cell(e - 2)
        for c in range(5):
            DR[c, 0, e] = fn[c] - f[c]
            DR[c, 1, e] = un[c] - u[c]
            RF[c, e] = fn[c] + f[c]
        SR[e] = jnp.maximum(s, sn)
        return (*un, *fn, sn)

    u, f, s = cell(0)
    for c in range(5):
        RF[c, 2] = f[c] + f[c]
    SR[2] = s
    last = lax.fori_loop(3, rows + 2, edge, (*u, *f, s))
    for c in range(5):
        RF[c, rows + 2] = last[5 + c] + last[5 + c]
    SR[rows + 2] = last[10]

    def face(c, e):
        df = [DR[c, 0, e + k] for k in range(-2, 3)]
        du = [DR[c, 1, e + k] for k in range(-2, 3)]
        return face_flux12(df, du, SR[e], RF[c, e])

    for c in range(5):
        LF[c] = face(c, 2)

    gain = SECTION_GAIN * TIME_STEP

    def one_row(r, _):
        row = r.astype(jnp.float32)
        radius = INNER_RADIUS + RADIAL_STEP * (row + 0.5)
        rr = 1.0 / jnp.full((1, 1, 128), radius, jnp.float32)
        k_low = (gain / 12.0 / RADIAL_STEP) * (INNER_RADIUS + RADIAL_STEP * row) * rr
        k_up = (gain / 12.0 / RADIAL_STEP) * (INNER_RADIUS + RADIAL_STEP * (row + 1.0)) * rr
        k_src = gain * rr
        for c in range(5):
            up = face(c, r + 3)
            value = k_low * LF[c] - k_up * up
            LF[c] = up
            value = value + (SECTION_KEEP * tiles(start, c, r, every) + SECTION_GAIN * tiles(state, c, r, every))
            if c == 1:
                value = value + k_src * S1[r]
            if c == 2:
                value = value - k_src * S2[r]
            for l in range(lt):
                part[c, r, :, 128 * l:128 * l + 128] = value[l]
        return 0

    lax.fori_loop(0, rows, one_row, 0)

    @pl.when(i == nblk - 1)
    def _():
        for cp in cycle_copies():
            cp.wait()
        from_az[me_a] = line_sum[...]
        total[...] = ordered_sum(from_az, na)

        def finish(b, _):
            for cp in pack_copies(b):
                cp.wait()
            for j in range(per_turn):
                for cp in end_copies(b * per_turn + j):
                    cp.wait()
            return 0

        lax.fori_loop(0, turns, finish, 0)


def radial_part(state, start, sums, na, nx):
    _, rows, stations, cells = state.shape
    lt = cells // 128
    nblk = stations // SB
    f32 = jnp.float32
    spec = pl.BlockSpec((5, rows, SB, cells), lambda i: (0, 0, i, 0))
    low_spec = pl.BlockSpec((5, rows, SB, cells), lambda i: (0, 0, 0, 0))
    high_spec = pl.BlockSpec((5, rows, SB, cells), lambda i: (0, 0, nblk - 1, 0))
    small = pl.BlockSpec((SB, 128), lambda i: (0, 0))
    any_spec = pl.BlockSpec(memory_space=pl.ANY)
    turns = nblk // 2
    far = lt - 1
    head_spec = pl.BlockSpec((5, rows, 2 * SB, 128), lambda i: (0, 0, i % turns, 0))
    tail_spec = pl.BlockSpec((5, rows, 2 * SB, 128), lambda i: (0, 0, i % turns, far))
    side = jax.ShapeDtypeStruct((turns, 5, 2 * SB, 128), f32)
    end = jax.ShapeDtypeStruct((5, rows, SB, cells), f32)
    dma = pltpu.SemaphoreType.DMA
    return pl.pallas_call(
        functools.partial(radial_kernel, rows, lt, na, nx),
        out_shape=(jax.ShapeDtypeStruct(state.shape, f32), side, side, end, end,
                   jax.ShapeDtypeStruct((SB, 128), f32)),
        grid=(nblk,),
        in_specs=[spec, spec, head_spec, tail_spec, low_spec, high_spec, pl.BlockSpec((GORES,), lambda i: (0,))],
        out_specs=(spec,) + (any_spec,) * 4 + (small,),
        scratch_shapes=[
            pltpu.VMEM((5, 2, rows + 5, lt, SB, 128), f32),
            pltpu.VMEM((rows + 5, lt, SB, 128), f32),
            pltpu.VMEM((5, rows + 5, lt, SB, 128), f32),
            pltpu.VMEM((5, lt, SB, 128), f32),
            pltpu.VMEM((rows, lt, SB, 128), f32),
            pltpu.VMEM((rows, lt, SB, 128), f32),
            pltpu.VMEM((turns, 5, 2 * SB, 128), f32),
            pltpu.VMEM((SB, 128), f32),
            pltpu.VMEM((nx, SB, 128), f32),
            pltpu.VMEM((na, SB, 128), f32),
            pltpu.VMEM((SB, 128), f32),
            dma((2, rows)), dma((2, rows)), dma((2, turns)), dma((2, turns)),
            dma((nx - 1,)), dma((nx - 1,)), dma((na - 1,)), dma((na - 1,)),
        ],
        compiler_params=pltpu.CompilerParams(
            dimension_semantics=("arbitrary",), collective_id=0, has_side_effects=True,
            vmem_limit_bytes=63 << 20),
        cost_estimate=pl.CostEstimate(
            flops=state.size * 90, bytes_accessed=state.size * 12, transcendentals=0),
        name="radial_part",
    )(state, start, state, state, state, state, sums)


def row_step(i, r0, count, lt, nblk, blocks, out, scratch):
    state, ahead, lo, hi, left, right, part = blocks
    U, F, DF, DU, FF, SX, UZ, FZ, DFZ, DUZ, FFZ, SZ, TZ, AZ, LT, RT = scratch
    st = nblk * SB
    cells = lt * 128
    nz = cells // SB
    step = 2 * SB
    turns = cells // step
    per_turn = nblk // turns
    per_line = nz // nblk
    lr = i + r0
    every = slice(None)
    sub = lax.broadcasted_iota(jnp.int32, (SB, 128), 0)

    line = lax.axis_index("ax")
    at_low = line == 0
    at_high = line == lax.axis_size("ax") - 1

    def block(b):
        return pl.ds(b * SB if isinstance(b, int) else pl.multiple_of(b * SB, SB), SB)

    def line_cells(u, b):
        rinv, p, cs = primitives(u)
        vel = u[3] * rinv
        f = fluxes(u, vel, p, 3)
        ds = block(b)
        for c in range(5):
            U[c, :, ds, :] = u[c]
            F[c, :, ds, :] = f[c]
        SX[:, ds, :] = jnp.abs(vel) + cs

    def line_end(ref, at_end, b, edge, to):
        u = []
        for c in range(5):
            inner = tiles(state, c, block(b))[:, edge:edge + 1]
            u.append(jnp.where(at_end, jnp.broadcast_to(inner, (lt, SB, 128)), tiles(ref, c, every)))
        line_cells(u, to)

    def line_block(b):
        line_cells([tiles(state, c, block(b)) for c in range(5)], b + 1)

    def turned_tile(src, t):
        c, l = t // lt, t % lt
        at = 128 * l
        if not isinstance(t, int):
            at = pl.multiple_of(at, 128)
        UZ[c, 0, pl.ds(at + SB, 128), :] = src[c, :, pl.ds(at, 128)].T

    def cycle_ends(row):
        for c in range(5):
            UZ[c, 0, pl.ds(0, SB), :] = pltpu.roll(LT[c, block(row), :], 5, 0)
            UZ[c, 0, pl.ds(SB + cells, SB), :] = pltpu.roll(RT[c, block(row), :], 5, 0)

    def cycle_cells(b):
        ds = block(b)
        u = [UZ[c, :, ds, :] for c in range(5)]
        rinv, p, cs = primitives(u)
        vel = u[2] * rinv
        f = fluxes(u, vel, p, 2)
        for c in range(5):
            FZ[c, :, ds, :] = f[c]
        SZ[:, ds, :] = jnp.abs(vel) + cs

    lines = ((F, DF), (U, DU))
    cycles = ((FZ, DFZ), (UZ, DUZ))

    def diff_block(pairs, b):
        o = b * SB if isinstance(b, int) else pl.multiple_of(b * SB, SB)
        for X, D in pairs:
            for c in range(5):
                D[c, :, pl.ds(o, SB), :] = X[c, :, pl.ds(o + 1, SB), :] - X[c, :, pl.ds(o, SB), :]

    def diff_last(pairs, b):
        for X, D in pairs:
            for c in range(5):
                x = X[c, :, block(b), :]
                D[c, :, block(b), :] = pltpu.roll(x, SB - 1, 1) - x

    def faces(F, DF, DU, S, c, base, n):
        df = [DF[c, :, pl.ds(base + k, n), :] for k in range(-2, 3)]
        du = [DU[c, :, pl.ds(base + k, n), :] for k in range(-2, 3)]
        a = jnp.maximum(S[:, pl.ds(base, n), :], S[:, pl.ds(base + 1, n), :])
        return face_flux12(df, du, a, F[c, :, pl.ds(base, n), :] + F[c, :, pl.ds(base + 1, n), :])

    def first_faces(F, DF, DU, S, FF):
        e = SB - 1
        for l in range(F.shape[1]):
            def pick(X, k):
                x = X[0, l, pl.ds(e + k, SB), :]
                for c in range(1, 5):
                    x = jnp.where(sub == c, X[c, l, pl.ds(e + k - c, SB), :], x)
                return x

            df = [pick(DF, k) for k in range(-2, 3)]
            du = [pick(DU, k) for k in range(-2, 3)]
            a = jnp.maximum(S[l, pl.ds(e, 1), :], S[l, pl.ds(e + 1, 1), :])
            f = face_flux12(df, du, a, pick(F, 0) + pick(F, 1))
            for c in range(5):
                FF[c, l, pl.ds(e, 1), :] = f[c:c + 1]

    gain = SECTION_GAIN * TIME_STEP
    radius = INNER_RADIUS + RADIAL_STEP * (lr.astype(jnp.float32) + 0.5)
    rr = 1.0 / jnp.full((1, 1, 128), radius, jnp.float32)
    k_cycle = (gain / 12.0 * NA / (2.0 * math.pi)) * rr
    k_line = gain / 12.0 / AXIAL_STEP

    @pl.when(i == 0)
    def _():
        for c in range(5):
            LT[c] = left[:, c].reshape(st, 128).T
            RT[c] = right[:, c].reshape(st, 128).T
        for t in range(5 * lt):
            turned_tile(state, t)
        cycle_ends(lr)

        def cells_loop(b, _):
            cycle_cells(b)
            return 0

        def diff_loop(b, _):
            diff_block(cycles, b)
            return 0

        lax.fori_loop(0, nz + 2, cells_loop, 0)
        lax.fori_loop(0, nz + 1, diff_loop, 0)
        diff_last(cycles, nz + 1)
        first_faces(FZ, DFZ, DUZ, SZ, FFZ)

    def cycle_turn(b, _):
        base = pl.multiple_of(b * step + SB, SB)
        for c in range(5):
            fa = faces(FZ, DFZ, DUZ, SZ, c, base, step)
            FFZ[c, :, pl.ds(base, step), :] = fa
            TZ[c, pl.ds(pl.multiple_of(b * step, step), step), :] = (
                k_cycle * (FFZ[c, :, pl.ds(base - 1, step), :] - fa))[0]
        for j in range(per_turn):
            diff_block(lines, jnp.maximum(per_turn * b - per_turn + j, 0))
        for j in range(per_turn):
            line_block(per_turn * b + j)
        turned_tile(ahead, jnp.minimum(b, 5 * lt - 1))
        return 0

    lax.fori_loop(0, turns, cycle_turn, 0)

    line_end(lo, at_low, 0, 0, 0)
    line_end(hi, at_high, nblk - 1, SB - 1, nblk + 1)
    diff_block(lines, 0)
    for b in range(nblk - per_turn, nblk + 1):
        diff_block(lines, b)
    diff_last(lines, nblk + 1)
    first_faces(F, DF, DU, SX, FF)
    for c in range(5):
        for l in range(lt):
            AZ[c, l] = TZ[c, pl.ds(128 * l, 128), :].T
    cycle_ends(r0 + (i + 1) % count)

    def line_turn(b, _):
        hs = block(b)
        base = pl.multiple_of(b * SB + SB, SB)
        for c in range(5):
            fx = faces(F, DF, DU, SX, c, base, SB)
            FF[c, :, pl.ds(base, SB), :] = fx
            delta = k_line * (FF[c, :, pl.ds(base - 1, SB), :] - fx) + AZ[c, :, hs, :]
            for l in range(lt):
                ls = slice(128 * l, 128 * l + 128)
                value = part[c, hs, ls] + delta[l]
                out[c, hs, ls] = value
        for j in range(per_line):
            diff_block(cycles, jnp.maximum(per_line * b - per_line - 1 + j, 0))
        for j in range(per_line):
            cycle_cells(per_line * b + j)
        return 0

    lax.fori_loop(0, nblk, line_turn, 0)

    cycle_cells(nz)
    cycle_cells(nz + 1)
    for b in range(nz - per_line - 1, nz + 1):
        diff_block(cycles, b)
    diff_last(cycles, nz + 1)
    first_faces(FZ, DFZ, DUZ, SZ, FFZ)


def send_kernel(count, middle, lt, nblk, na, *refs):
    blocks, (cutoff, near_rows), source = refs[:7], refs[7:9], refs[9:13]
    out, final = refs[13:15]
    scratch = refs[15:31]
    (near, spread, kept, coef, tables, turned,
     near_send, near_recv, near_own, kept_send, kept_recv, fetch) = refs[31:]
    share = spread.shape[3]
    i = pl.program_id(0)
    me = lax.axis_index("az")
    MESH = pl.DeviceIdType.MESH

    def peer(d):
        return lax.rem(me + d, na)

    def remote(src, dst, send, recv, d):
        return pltpu.make_async_remote_copy(
            src_ref=src, dst_ref=dst, send_sem=send, recv_sem=recv,
            device_id={"az": peer(d)}, device_id_type=MESH)

    def stations_of(g):
        return pl.ds(pl.multiple_of(g * share, SB), share)

    def near_copies(j):
        return [
            remote(near.at[j, :, stations_of(peer(d)), :], spread.at[me, :, j],
                   near_send.at[d - 1, j], near_recv.at[d - 1, j], d)
            for d in range(1, na)
        ] + [pltpu.make_async_copy(near.at[j, :, stations_of(me), :], spread.at[me, :, j], near_own.at[j])]

    def kept_copies():
        return [
            remote(kept.at[peer(d)], final.at[me], kept_send.at[d - 1], kept_recv.at[d - 1], d)
            for d in range(1, na)
        ] + [pltpu.make_async_copy(kept.at[me], final.at[me], near_own.at[NF])]

    def table_copies():
        return [pltpu.make_async_copy(source[t], tables.at[t], fetch.at[t]) for t in range(4)]

    @pl.when(i == 0)
    def _():
        barrier = pltpu.get_barrier_semaphore()
        for d in range(1, na):
            pl.semaphore_signal(barrier, inc=1, device_id={"az": peer(d)}, device_id_type=MESH)
        for cp in table_copies():
            cp.start()

    @pl.when(i == 1)
    def _():
        pl.semaphore_wait(pltpu.get_barrier_semaphore(), na - 1)

    @pl.when((i >= 1) & (i <= NF))
    def _():
        for cp in near_copies(i - 1):
            cp.start()

    @pl.when(i == middle)
    def _():
        for cp in table_copies():
            cp.wait()
        for j in range(NF):
            for cp in near_copies(j):
                cp.wait()
        low_pass(spread, kept, coef, tables, turned, cutoff, near_rows)
        for cp in kept_copies():
            cp.start()

    row_step(i, 0, count, lt, nblk, blocks, out, scratch)

    @pl.when(i < NF)
    def _():
        for c in range(5):
            near[i, c] = out[c]

    @pl.when(i == count - 1)
    def _():
        for cp in kept_copies():
            cp.wait()


def join_kernel(r0, count, lt, nblk, na, *refs):
    blocks, (whole, final, loads) = refs[:7], refs[7:10]
    result, gores = refs[10:12]
    scratch = refs[12:28]
    row_out, stage, stage_near, row_sem, come, go, come_near, go_near = refs[28:]
    share = stage_near.shape[3]
    i = pl.program_id(0)

    def in_copies():
        return [pltpu.make_async_copy(whole.at[:, r], stage.at[r - NF], come.at[r - NF])
                for r in range(NF, r0)] + [
            pltpu.make_async_copy(final.at[g], stage_near.at[g], come_near.at[g]) for g in range(na)]

    def out_copies():
        return [pltpu.make_async_copy(stage.at[r - NF], result.at[:, r], go.at[r - NF])
                for r in range(NF, r0)] + [
            pltpu.make_async_copy(
                stage_near.at[g], result.at[:, pl.ds(0, NF), pl.ds(g * share, share), :], go_near.at[g])
            for g in range(na)]

    def row_copy(j):
        return pltpu.make_async_copy(row_out.at[j], result.at[:, r0 + j], row_sem.at[j])

    @pl.when(i == 0)
    def _():
        gores[...] = loads[0:1, 0:GORES].reshape(GORES)
        for cp in in_copies():
            cp.start()

    @pl.when(i == 1)
    def _():
        for cp in in_copies():
            cp.wait()
        for cp in out_copies():
            cp.start()

    row_step(i, r0, count, lt, nblk, blocks, row_out.at[i], scratch)
    row_copy(i).start()

    @pl.when(i == count - 1)
    def _():
        for cp in out_copies():
            cp.wait()
        for j in range(count):
            row_copy(j).wait()


def row_call(kernel, name, r0, count, args, extra, extra_specs, out_shape, out_specs, more, **params):
    state = args[0]
    _, rows, stations, cells = state.shape
    lt = cells // 128
    nblk = stations // SB
    f32 = jnp.float32
    row_spec = pl.BlockSpec((5, None, stations, cells), lambda i: (0, r0 + i, 0, 0))
    ahead_spec = pl.BlockSpec((5, None, stations, cells), lambda i: (0, r0 + (i + 1) % count, 0, 0))
    end_spec = pl.BlockSpec((5, None, SB, cells), lambda i: (0, r0 + i, 0, 0))
    pack_spec = pl.BlockSpec((nblk // 2, 5, 2 * SB, 128), lambda i: (0, 0, 0, 0))
    field = pltpu.VMEM((lt, stations + 2 * SB, 128), f32)
    group = pltpu.VMEM((5, lt, stations + 2 * SB, 128), f32)
    field_z = pltpu.VMEM((1, cells + 2 * SB, stations), f32)
    group_z = pltpu.VMEM((5, 1, cells + 2 * SB, stations), f32)
    return pl.pallas_call(
        kernel,
        out_shape=out_shape,
        grid=(count,),
        in_specs=[row_spec, ahead_spec, end_spec, end_spec, pack_spec, pack_spec, row_spec] + extra_specs,
        out_specs=out_specs(row_spec),
        scratch_shapes=[group] * 5 + [field] + [group_z] * 5 + [
            field_z,
            pltpu.VMEM((5, cells, stations), f32),
            pltpu.VMEM((5, lt, stations, 128), f32),
            pltpu.VMEM((5, 128, stations), f32),
            pltpu.VMEM((5, 128, stations), f32),
        ] + more,
        compiler_params=pltpu.CompilerParams(
            dimension_semantics=("arbitrary",), vmem_limit_bytes=63 << 20, **params),
        name=name,
    )(state, *args, *extra)


def rk_rows(state, lo, hi, left, right, part, cutoff, near_rows, loads, na):
    _, rows, stations, cells = state.shape
    lt = cells // 128
    nblk = stations // SB
    share = stations // na
    f32 = jnp.float32
    count = rows - 2
    middle = NF + 2 * (count - NF) // 5
    args = [state, lo, hi, left, right, part]
    any_spec = pl.BlockSpec(memory_space=pl.ANY)
    shape = (na, 5, NF, share, cells)
    pieces = pltpu.VMEM(shape, f32)
    whole_shape = jax.ShapeDtypeStruct(state.shape, f32)
    dma = pltpu.SemaphoreType.DMA
    whole, final = row_call(
        functools.partial(send_kernel, count, middle, lt, nblk, na), "rows_send", 0, count, args,
        [cutoff, near_rows[None], *(jnp.asarray(t) for t in mode_tables())],
        [pl.BlockSpec(cutoff.shape, lambda i: (0, 0)), pl.BlockSpec((1, stations), lambda i: (0, 0))]
        + [any_spec] * 4,
        (whole_shape, jax.ShapeDtypeStruct(shape, f32)),
        lambda row_spec: (row_spec, any_spec),
        [
            pltpu.VMEM((NF, 5, stations, cells), f32),
            pieces, pieces,
            pltpu.VMEM((2, 5 * NF * share, NA // 4), f32),
            pltpu.VMEM((4, NA // 2, NA // 4), jnp.bfloat16),
            pltpu.VMEM((stations, 2 * NF), f32),
            dma((na - 1, NF)), dma((na - 1, NF)), dma((NF + 1,)),
            dma((na - 1,)), dma((na - 1,)), dma((4,)),
        ],
        collective_id=1, has_side_effects=True)
    return row_call(
        functools.partial(join_kernel, count, rows - count, lt, nblk, na), "rows_join",
        count, rows - count, args,
        [whole, final, loads],
        [any_spec, any_spec, pl.BlockSpec((SB, 128), lambda i: (0, 0))],
        (whole_shape, jax.ShapeDtypeStruct((GORES,), f32)),
        lambda row_spec: (any_spec, pl.BlockSpec((GORES,), lambda i: (0,))),
        [
            pltpu.VMEM((rows - count, 5, stations, cells), f32),
            pltpu.VMEM((count - NF, 5, stations, cells), f32),
            pieces,
            dma((rows - count,)), dma((count - NF,)), dma((count - NF,)), dma((na,)), dma((na,)),
        ])


def mode_tables():
    n = np.arange(NA // 2)[:, None]
    tables = []
    for parity in (0, 1):
        k = np.arange(parity, NA // 4, 2)[None, :]
        angle = 2.0 * math.pi / NA * ((n * k) % NA)
        table = np.concatenate([np.cos(angle), np.sin(angle)], axis=1).astype(np.float32)
        high = table.astype(jnp.bfloat16)
        tables += [high, (table - high.astype(np.float32)).astype(jnp.bfloat16)]
    return tables


def split(x):
    high = x.astype(jnp.bfloat16)
    return high, (x - high.astype(jnp.float32)).astype(jnp.bfloat16)


def product(x, y, dims):
    x_high, x_low = x
    y_high, y_low = y

    def dot(a, b):
        return lax.dot_general(a, b, (dims, ((), ())), preferred_element_type=jnp.float32)

    return dot(x_high, y_high) + (dot(x_low, y_high) + dot(x_high, y_low))


def low_pass(x, out, coef, tables, turned, cutoff, near_rows):
    pieces, _, _, share, cells = x.shape
    m = 5 * NF * share
    half = pieces // 2
    modes = tables.shape[2] // 2
    chosen = lax.broadcasted_iota(jnp.int32, cutoff.shape, 0) < near_rows[...]
    signed = jnp.where(chosen, cutoff[...], -cutoff[...]).astype(jnp.float32)
    turned[...] = jnp.concatenate([signed, signed], axis=0).T
    here = turned[pl.ds(pl.multiple_of(lax.axis_index("az") * share, SB), share), :]
    signs = jnp.concatenate([here[:, j:j + 1] for j in range(NF)] * 5, axis=0)
    limit = jnp.abs(signs).astype(jnp.int32)
    take = signs > 0.0

    for p in range(half):
        x0 = x[p].reshape(m, cells)
        x1 = x[p + half].reshape(m, cells)
        at = slice(p * cells, (p + 1) * cells)
        for parity, part in enumerate((x0 + x1, x0 - x1)):
            rhs = (tables[2 * parity, at, :], tables[2 * parity + 1, at, :])
            value = product(split(part), rhs, ((1,), (0,)))
            coef[parity] = value if p == 0 else coef[parity] + value
    column = lax.broadcasted_iota(jnp.int32, (m, 2 * modes), 1)
    column = jnp.where(column < modes, column, column - modes)
    back = []
    for parity in range(2):
        k = 2 * column + parity
        weight = jnp.where(k == 0, 1.0 / NA, 2.0 / NA)
        gains = jnp.where(k < limit, weight, 0.0)
        back.append(split(coef[parity] * gains))
    for p in range(half):
        at = slice(p * cells, (p + 1) * cells)
        y0, y1 = (
            product(back[parity], (tables[2 * parity, at, :], tables[2 * parity + 1, at, :]), ((1,), (1,)))
            for parity in range(2)
        )
        for q, y in ((p, y0 + y1), (p + half, y0 - y1)):
            kept = jnp.where(take, y, x[q].reshape(m, cells))
            out[q] = kept.reshape(5, NF, share, cells)


def pressure_of(conserved):
    density = conserved[0]
    kinetic = (
        0.5
        * (conserved[1] * conserved[1] + conserved[2] * conserved[2] + conserved[3] * conserved[3])
        / density
    )
    return (HEAT_RATIO - 1.0) * (conserved[4] - kinetic)


def per_device(step_start, section_state, near_rows, cutoff, gore_map):
    _, rows, stations, cells = section_state.shape
    na, nx = lax.axis_size("az"), lax.axis_size("ax")
    line_index = lax.axis_index("ax")
    canopy = rows // 2
    jump = pressure_of(section_state[:, canopy - 1]) - pressure_of(section_state[:, canopy + 1])
    total = stations * nx
    station = line_index * stations + jnp.arange(stations, dtype=jnp.int32)
    ramp = 1.0 + 2.0 * station.astype(jnp.float32) / total
    weighted = jump * ramp[:, None] * (1.0 / math.sqrt(total * NA / GORES))
    gores = jnp.arange(GORES, dtype=jnp.int32)
    partial = jnp.sum(
        jnp.where(gore_map[None] == gores[:, None, None], weighted[None], 0.0), axis=(1, 2))
    part, left, right, lo, hi, loads = radial_part(section_state, step_start, partial, na, nx)

    return tuple(rk_rows(
        section_state, lo, hi, left, right, part, cutoff, near_rows, loads, na))


def solution(mesh):
    in_specs = (
        P(None, None, "ax", "az"),
        P(None, None, "ax", "az"),
        P("ax"),
        P(None, "ax"),
        P("ax", "az"),
    )
    out_specs = (P(None, None, "ax", "az"), P())
    return jax.shard_map(
        per_device, mesh=mesh, in_specs=in_specs, out_specs=out_specs, check_vma=False
    )
```

```python
import functools
import math

import jax
import jax.numpy as jnp
import numpy as np
from jax import lax
from jax.experimental import pallas as pl
from jax.experimental.pallas import tpu as pltpu
from jax.sharding import PartitionSpec as P

NA = 2048
NF = 4
GORES = 80

HEAT_RATIO = 1.4
WEIGHT_EPSILON = 1e-06
INNER_RADIUS = 24.0
RADIAL_STEP = 0.5
AXIAL_STEP = 0.5
TIME_STEP = 0.01
SECTION_KEEP = 1.0 / 3.0
SECTION_GAIN = 2.0 / 3.0

SB = 8
BEGIN = 3
EPS = 3.0 * WEIGHT_EPSILON


def side(d1, d2, d3, d4):
    e1 = d2 - d1
    e2 = d3 - d2
    e3 = d4 - d3
    h2 = 0.75 * d2
    h3 = 0.75 * d3
    g2 = h2 * d2 + EPS
    g3 = h3 * d3 + EPS
    s1 = e1 * (e1 + h2) + g2
    s2 = e2 * (e2 + h2) + g2
    s3 = e3 * (e3 - h3) + g3
    t1 = s2 * pl.reciprocal(s1, approx=False)
    t3 = s2 * pl.reciprocal(s3, approx=False)
    w1 = t1 * t1
    w3 = 3.0 * (t3 * t3)
    num = (w1 + w1) * (e1 - e2) + w3 * (e2 - e3)
    return num * pl.reciprocal((w1 + 6.0) + w3, approx=False), e2


def face_flux12(df, du, a, fsum):
    au = [a * x for x in du]
    pm2, pm1, p0, p1 = (df[k] + au[k] for k in range(4))
    mm1, m0, m1, m2 = (df[k] - au[k] for k in range(1, 5))
    cp, ep = side(pm2, pm1, p0, p1)
    cm, em = side(m2, m1, m0, mm1)
    return 6.0 * fsum + ((cp - cm) - (ep - em))


def primitives(u):
    rinv = 1.0 / u[0]
    kin = 0.5 * (u[1] * u[1] + u[2] * u[2] + u[3] * u[3]) * rinv
    p = (HEAT_RATIO - 1.0) * (u[4] - kin)
    cs = jnp.sqrt(HEAT_RATIO * p * rinv)
    return rinv, p, cs


def fluxes(u, vel, p, normal):
    f = [u[normal], u[1] * vel, u[2] * vel, u[3] * vel, (u[4] + p) * vel]
    f[normal] = f[normal] + p
    return f


def tiles(ref, *ix):
    cells = ref.shape[-1]
    return jnp.stack([ref[(*ix, slice(128 * l, 128 * l + 128))] for l in range(cells // 128)])


def radial_kernel(rows, lt, na, nx, state, start, head, tail, low_end, high_end, sums,
                  part, left, right, lo, hi, total,
                  DR, SR, RF, LF, S1, S2, pack, own, from_ax, from_az, line_sum,
                  end_send, end_recv, pack_send, pack_recv, ax_send, ax_recv, az_send, az_recv):
    i = pl.program_id(0)
    every = slice(None)
    me_a, me_x = lax.axis_index("az"), lax.axis_index("ax")
    turns = pack.shape[0]
    nblk = 2 * turns
    per_turn = rows // turns
    assert per_turn * turns == rows
    MESH = pl.DeviceIdType.MESH

    def peer_a(d):
        return {"az": lax.rem(me_a + d, na)}

    def peer_x(d):
        return {"ax": lax.rem(me_x + d, nx)}

    def copy(src, dst, send, recv, peer):
        return pltpu.make_async_remote_copy(
            src_ref=src, dst_ref=dst, send_sem=send, recv_sem=recv,
            device_id=peer, device_id_type=MESH)

    def end_copies(r):
        return [
            copy(high_end.at[:, r], lo.at[:, r], end_send.at[0, r], end_recv.at[0, r], peer_x(1)),
            copy(low_end.at[:, r], hi.at[:, r], end_send.at[1, r], end_recv.at[1, r], peer_x(nx - 1)),
        ]

    def pack_copies(b):
        return [
            copy(pack.at[b], left.at[b], pack_send.at[0, b], pack_recv.at[0, b], peer_a(1)),
            copy(pack.at[b], right.at[b], pack_send.at[1, b], pack_recv.at[1, b], peer_a(na - 1)),
        ]

    def line_copies():
        return [
            copy(own, from_ax.at[me_x], ax_send.at[d], ax_recv.at[d], peer_x(d + 1))
            for d in range(nx - 1)
        ]

    def cycle_copies():
        return [
            copy(line_sum, from_az.at[me_a], az_send.at[d], az_recv.at[d], peer_a(d + 1))
            for d in range(na - 1)
        ]

    def ordered_sum(ref, count):
        value = ref[0]
        for d in range(1, count):
            value = value + ref[d]
        return value

    @pl.when(i == 0)
    def _():
        barrier = pltpu.get_barrier_semaphore()
        for d in range(1, na):
            pl.semaphore_signal(barrier, inc=1, device_id=peer_a(d), device_id_type=MESH)
        for d in range(1, nx):
            pl.semaphore_signal(barrier, inc=1, device_id=peer_x(d), device_id_type=MESH)
        own[...] = jnp.zeros((SB, 128), jnp.float32)
        own[0:1, 0:GORES] = sums[...].reshape(1, GORES)
        for e in (0, 1, 2, rows + 2, rows + 3, rows + 4):
            DR[:, :, e] = jnp.zeros((5, 2, lt, SB, 128), jnp.float32)

    lane = lax.broadcasted_iota(jnp.int32, (2 * SB, 128), 1)
    near_side = lane < 64
    owner = lane // 8

    @pl.when(i < turns)
    def _():
        for c in range(5):
            value = None
            for q in range(rows):
                ends = pltpu.roll(jnp.where(near_side, head[c, q], tail[c, q]), (8 * q + 3) % 128, 1)
                value = ends if q == 0 else jnp.where(owner == q, ends, value)
            pack[i, c] = value

    @pl.when(i == BEGIN)
    def _():
        pl.semaphore_wait(pltpu.get_barrier_semaphore(), na + nx - 2)
        for cp in line_copies():
            cp.start()

    @pl.when((i >= BEGIN) & (i < BEGIN + turns))
    def _():
        b = i - BEGIN
        for cp in pack_copies(b):
            cp.start()
        for j in range(per_turn):
            for cp in end_copies(b * per_turn + j):
                cp.start()

    @pl.when(i == BEGIN + nblk // 4)
    def _():
        for cp in line_copies():
            cp.wait()
        from_ax[me_x] = own[...]
        line_sum[...] = ordered_sum(from_ax, nx)
        for cp in cycle_copies():
            cp.start()

    def cell(q):
        u = [tiles(state, c, q, every) for c in range(5)]
        rinv, p, cs = primitives(u)
        vel = u[1] * rinv
        swirl = u[2] * rinv
        S1[q] = u[2] * swirl + p
        S2[q] = u[1] * swirl
        return u, fluxes(u, vel, p, 1), jnp.abs(vel) + cs

    def edge(e, carry):
        u, f, s = carry[:5], carry[5:10], carry[10]
        un, fn, sn = cell(e - 2)
        for c in range(5):
            DR[c, 0, e] = fn[c] - f[c]
            DR[c, 1, e] = un[c] - u[c]
            RF[c, e] = fn[c] + f[c]
        SR[e] = jnp.maximum(s, sn)
        return (*un, *fn, sn)

    u, f, s = cell(0)
    for c in range(5):
        RF[c, 2] = f[c] + f[c]
    SR[2] = s
    last = lax.fori_loop(3, rows + 2, edge, (*u, *f, s))
    for c in range(5):
        RF[c, rows + 2] = last[5 + c] + last[5 + c]
    SR[rows + 2] = last[10]

    def face(c, e):
        df = [DR[c, 0, e + k] for k in range(-2, 3)]
        du = [DR[c, 1, e + k] for k in range(-2, 3)]
        return face_flux12(df, du, SR[e], RF[c, e])

    for c in range(5):
        LF[c] = face(c, 2)

    gain = SECTION_GAIN * TIME_STEP

    def one_row(r, _):
        row = r.astype(jnp.float32)
        radius = INNER_RADIUS + RADIAL_STEP * (row + 0.5)
        rr = 1.0 / jnp.full((1, 1, 128), radius, jnp.float32)
        k_low = (gain / 12.0 / RADIAL_STEP) * (INNER_RADIUS + RADIAL_STEP * row) * rr
        k_up = (gain / 12.0 / RADIAL_STEP) * (INNER_RADIUS + RADIAL_STEP * (row + 1.0)) * rr
        k_src = gain * rr
        for c in range(5):
            up = face(c, r + 3)
            value = k_low * LF[c] - k_up * up
            LF[c] = up
            value = value + (SECTION_KEEP * tiles(start, c, r, every) + SECTION_GAIN * tiles(state, c, r, every))
            if c == 1:
                value = value + k_src * S1[r]
            if c == 2:
                value = value - k_src * S2[r]
            for l in range(lt):
                part[c, r, :, 128 * l:128 * l + 128] = value[l]
        return 0

    lax.fori_loop(0, rows, one_row, 0, unroll=2)

    @pl.when(i == nblk - 1)
    def _():
        for cp in cycle_copies():
            cp.wait()
        from_az[me_a] = line_sum[...]
        total[...] = ordered_sum(from_az, na)

        def finish(b, _):
            for cp in pack_copies(b):
                cp.wait()
            for j in range(per_turn):
                for cp in end_copies(b * per_turn + j):
                    cp.wait()
            return 0

        lax.fori_loop(0, turns, finish, 0)


def radial_part(state, start, sums, na, nx):
    _, rows, stations, cells = state.shape
    lt = cells // 128
    nblk = stations // SB
    f32 = jnp.float32
    spec = pl.BlockSpec((5, rows, SB, cells), lambda i: (0, 0, i, 0))
    low_spec = pl.BlockSpec((5, rows, SB, cells), lambda i: (0, 0, 0, 0))
    high_spec = pl.BlockSpec((5, rows, SB, cells), lambda i: (0, 0, nblk - 1, 0))
    small = pl.BlockSpec((SB, 128), lambda i: (0, 0))
    any_spec = pl.BlockSpec(memory_space=pl.ANY)
    turns = nblk // 2
    far = lt - 1
    head_spec = pl.BlockSpec((5, rows, 2 * SB, 128), lambda i: (0, 0, i % turns, 0))
    tail_spec = pl.BlockSpec((5, rows, 2 * SB, 128), lambda i: (0, 0, i % turns, far))
    side = jax.ShapeDtypeStruct((turns, 5, 2 * SB, 128), f32)
    end = jax.ShapeDtypeStruct((5, rows, SB, cells), f32)
    dma = pltpu.SemaphoreType.DMA
    return pl.pallas_call(
        functools.partial(radial_kernel, rows, lt, na, nx),
        out_shape=(jax.ShapeDtypeStruct(state.shape, f32), side, side, end, end,
                   jax.ShapeDtypeStruct((SB, 128), f32)),
        grid=(nblk,),
        in_specs=[spec, spec, head_spec, tail_spec, low_spec, high_spec, pl.BlockSpec((GORES,), lambda i: (0,))],
        out_specs=(spec,) + (any_spec,) * 4 + (small,),
        scratch_shapes=[
            pltpu.VMEM((5, 2, rows + 5, lt, SB, 128), f32),
            pltpu.VMEM((rows + 5, lt, SB, 128), f32),
            pltpu.VMEM((5, rows + 5, lt, SB, 128), f32),
            pltpu.VMEM((5, lt, SB, 128), f32),
            pltpu.VMEM((rows, lt, SB, 128), f32),
            pltpu.VMEM((rows, lt, SB, 128), f32),
            pltpu.VMEM((turns, 5, 2 * SB, 128), f32),
            pltpu.VMEM((SB, 128), f32),
            pltpu.VMEM((nx, SB, 128), f32),
            pltpu.VMEM((na, SB, 128), f32),
            pltpu.VMEM((SB, 128), f32),
            dma((2, rows)), dma((2, rows)), dma((2, turns)), dma((2, turns)),
            dma((nx - 1,)), dma((nx - 1,)), dma((na - 1,)), dma((na - 1,)),
        ],
        compiler_params=pltpu.CompilerParams(
            dimension_semantics=("arbitrary",), collective_id=0, has_side_effects=True,
            vmem_limit_bytes=63 << 20),
        cost_estimate=pl.CostEstimate(
            flops=state.size * 90, bytes_accessed=state.size * 12, transcendentals=0),
        name="radial_part",
    )(state, start, state, state, state, state, sums)


def row_step(i, r0, count, lt, nblk, blocks, out, scratch):
    state, ahead, lo, hi, left, right, part = blocks
    U, F, DF, DU, FF, SX, UZ, FZ, DFZ, DUZ, FFZ, SZ, TZ, AZ, LT, RT = scratch
    st = nblk * SB
    cells = lt * 128
    nz = cells // SB
    step = 2 * SB
    turns = cells // step
    per_turn = nblk // turns
    per_line = nz // nblk
    lr = i + r0
    every = slice(None)
    sub = lax.broadcasted_iota(jnp.int32, (SB, 128), 0)

    line = lax.axis_index("ax")
    at_low = line == 0
    at_high = line == lax.axis_size("ax") - 1

    def block(b):
        return pl.ds(b * SB if isinstance(b, int) else pl.multiple_of(b * SB, SB), SB)

    def line_cells(u, b):
        rinv, p, cs = primitives(u)
        vel = u[3] * rinv
        f = fluxes(u, vel, p, 3)
        ds = block(b)
        for c in range(5):
            U[c, :, ds, :] = u[c]
            F[c, :, ds, :] = f[c]
        SX[:, ds, :] = jnp.abs(vel) + cs

    def line_end(ref, at_end, b, edge, to):
        u = []
        for c in range(5):
            inner = tiles(state, c, block(b))[:, edge:edge + 1]
            u.append(jnp.where(at_end, jnp.broadcast_to(inner, (lt, SB, 128)), tiles(ref, c, every)))
        line_cells(u, to)

    def line_block(b):
        line_cells([tiles(state, c, block(b)) for c in range(5)], b + 1)

    def turned_tile(src, t):
        c, l = t // lt, t % lt
        at = 128 * l
        if not isinstance(t, int):
            at = pl.multiple_of(at, 128)
        UZ[c, 0, pl.ds(at + SB, 128), :] = src[c, :, pl.ds(at, 128)].T

    def cycle_ends(row):
        for c in range(5):
            UZ[c, 0, pl.ds(0, SB), :] = pltpu.roll(LT[c, block(row), :], 5, 0)
            UZ[c, 0, pl.ds(SB + cells, SB), :] = pltpu.roll(RT[c, block(row), :], 5, 0)

    def cycle_cells(b):
        ds = block(b)
        u = [UZ[c, :, ds, :] for c in range(5)]
        rinv, p, cs = primitives(u)
        vel = u[2] * rinv
        f = fluxes(u, vel, p, 2)
        for c in range(5):
            FZ[c, :, ds, :] = f[c]
        SZ[:, ds, :] = jnp.abs(vel) + cs

    lines = ((F, DF), (U, DU))
    cycles = ((FZ, DFZ), (UZ, DUZ))

    def diff_block(pairs, b):
        o = b * SB if isinstance(b, int) else pl.multiple_of(b * SB, SB)
        for X, D in pairs:
            for c in range(5):
                D[c, :, pl.ds(o, SB), :] = X[c, :, pl.ds(o + 1, SB), :] - X[c, :, pl.ds(o, SB), :]

    def diff_last(pairs, b):
        for X, D in pairs:
            for c in range(5):
                x = X[c, :, block(b), :]
                D[c, :, block(b), :] = pltpu.roll(x, SB - 1, 1) - x

    def faces(F, DF, DU, S, c, base, n):
        df = [DF[c, :, pl.ds(base + k, n), :] for k in range(-2, 3)]
        du = [DU[c, :, pl.ds(base + k, n), :] for k in range(-2, 3)]
        a = jnp.maximum(S[:, pl.ds(base, n), :], S[:, pl.ds(base + 1, n), :])
        return face_flux12(df, du, a, F[c, :, pl.ds(base, n), :] + F[c, :, pl.ds(base + 1, n), :])

    def first_faces(F, DF, DU, S, FF):
        e = SB - 1
        for l in range(F.shape[1]):
            def pick(X, k):
                x = X[0, l, pl.ds(e + k, SB), :]
                for c in range(1, 5):
                    x = jnp.where(sub == c, X[c, l, pl.ds(e + k - c, SB), :], x)
                return x

            df = [pick(DF, k) for k in range(-2, 3)]
            du = [pick(DU, k) for k in range(-2, 3)]
            a = jnp.maximum(S[l, pl.ds(e, 1), :], S[l, pl.ds(e + 1, 1), :])
            f = face_flux12(df, du, a, pick(F, 0) + pick(F, 1))
            for c in range(5):
                FF[c, l, pl.ds(e, 1), :] = f[c:c + 1]

    gain = SECTION_GAIN * TIME_STEP
    radius = INNER_RADIUS + RADIAL_STEP * (lr.astype(jnp.float32) + 0.5)
    rr = 1.0 / jnp.full((1, 1, 128), radius, jnp.float32)
    k_cycle = (gain / 12.0 * NA / (2.0 * math.pi)) * rr
    k_line = gain / 12.0 / AXIAL_STEP

    @pl.when(i == 0)
    def _():
        for c in range(5):
            LT[c] = left[:, c].reshape(st, 128).T
            RT[c] = right[:, c].reshape(st, 128).T
        for t in range(5 * lt):
            turned_tile(state, t)
        cycle_ends(lr)

        def cells_loop(b, _):
            cycle_cells(b)
            return 0

        def diff_loop(b, _):
            diff_block(cycles, b)
            return 0

        lax.fori_loop(0, nz + 2, cells_loop, 0)
        lax.fori_loop(0, nz + 1, diff_loop, 0)
        diff_last(cycles, nz + 1)
        first_faces(FZ, DFZ, DUZ, SZ, FFZ)

    def cycle_turn(b, _):
        base = pl.multiple_of(b * step + SB, SB)
        for c in range(5):
            fa = faces(FZ, DFZ, DUZ, SZ, c, base, step)
            FFZ[c, :, pl.ds(base, step), :] = fa
            TZ[c, pl.ds(pl.multiple_of(b * step, step), step), :] = (
                k_cycle * (FFZ[c, :, pl.ds(base - 1, step), :] - fa))[0]
        for j in range(per_turn):
            diff_block(lines, jnp.maximum(per_turn * b - per_turn + j, 0))
        for j in range(per_turn):
            line_block(per_turn * b + j)
        turned_tile(ahead, jnp.minimum(b, 5 * lt - 1))
        return 0

    lax.fori_loop(0, turns, cycle_turn, 0, unroll=2)

    line_end(lo, at_low, 0, 0, 0)
    line_end(hi, at_high, nblk - 1, SB - 1, nblk + 1)
    diff_block(lines, 0)
    for b in range(nblk - per_turn, nblk + 1):
        diff_block(lines, b)
    diff_last(lines, nblk + 1)
    first_faces(F, DF, DU, SX, FF)
    for c in range(5):
        for l in range(lt):
            AZ[c, l] = TZ[c, pl.ds(128 * l, 128), :].T
    cycle_ends(r0 + (i + 1) % count)

    def line_turn(b, _):
        hs = block(b)
        base = pl.multiple_of(b * SB + SB, SB)
        for c in range(5):
            fx = faces(F, DF, DU, SX, c, base, SB)
            FF[c, :, pl.ds(base, SB), :] = fx
            delta = k_line * (FF[c, :, pl.ds(base - 1, SB), :] - fx) + AZ[c, :, hs, :]
            for l in range(lt):
                ls = slice(128 * l, 128 * l + 128)
                value = part[c, hs, ls] + delta[l]
                out[c, hs, ls] = value
        for j in range(per_line):
            diff_block(cycles, jnp.maximum(per_line * b - per_line - 1 + j, 0))
        for j in range(per_line):
            cycle_cells(per_line * b + j)
        return 0

    lax.fori_loop(0, nblk, line_turn, 0, unroll=2)

    cycle_cells(nz)
    cycle_cells(nz + 1)
    for b in range(nz - per_line - 1, nz + 1):
        diff_block(cycles, b)
    diff_last(cycles, nz + 1)
    first_faces(FZ, DFZ, DUZ, SZ, FFZ)


def send_kernel(count, middle, lt, nblk, na, *refs):
    blocks, (cutoff, near_rows), source = refs[:7], refs[7:9], refs[9:13]
    out, final = refs[13:15]
    scratch = refs[15:31]
    (near, spread, kept, coef, tables, turned,
     near_send, near_recv, near_own, kept_send, kept_recv, fetch) = refs[31:]
    share = spread.shape[3]
    i = pl.program_id(0)
    me = lax.axis_index("az")
    MESH = pl.DeviceIdType.MESH

    def peer(d):
        return lax.rem(me + d, na)

    def remote(src, dst, send, recv, d):
        return pltpu.make_async_remote_copy(
            src_ref=src, dst_ref=dst, send_sem=send, recv_sem=recv,
            device_id={"az": peer(d)}, device_id_type=MESH)

    def stations_of(g):
        return pl.ds(pl.multiple_of(g * share, SB), share)

    def near_copies(j):
        return [
            remote(near.at[j, :, stations_of(peer(d)), :], spread.at[me, :, j],
                   near_send.at[d - 1, j], near_recv.at[d - 1, j], d)
            for d in range(1, na)
        ] + [pltpu.make_async_copy(near.at[j, :, stations_of(me), :], spread.at[me, :, j], near_own.at[j])]

    def kept_copies():
        return [
            remote(kept.at[peer(d)], final.at[me], kept_send.at[d - 1], kept_recv.at[d - 1], d)
            for d in range(1, na)
        ] + [pltpu.make_async_copy(kept.at[me], final.at[me], near_own.at[NF])]

    def table_copies():
        return [pltpu.make_async_copy(source[t], tables.at[t], fetch.at[t]) for t in range(4)]

    @pl.when(i == 0)
    def _():
        barrier = pltpu.get_barrier_semaphore()
        for d in range(1, na):
            pl.semaphore_signal(barrier, inc=1, device_id={"az": peer(d)}, device_id_type=MESH)
        for cp in table_copies():
            cp.start()

    @pl.when(i == 1)
    def _():
        pl.semaphore_wait(pltpu.get_barrier_semaphore(), na - 1)

    @pl.when((i >= 1) & (i <= NF))
    def _():
        for cp in near_copies(i - 1):
            cp.start()

    @pl.when(i == middle)
    def _():
        for cp in table_copies():
            cp.wait()
        for j in range(NF):
            for cp in near_copies(j):
                cp.wait()
        low_pass(spread, kept, coef, tables, turned, cutoff, near_rows)
        for cp in kept_copies():
            cp.start()

    row_step(i, 0, count, lt, nblk, blocks, out, scratch)

    @pl.when(i < NF)
    def _():
        for c in range(5):
            near[i, c] = out[c]

    @pl.when(i == count - 1)
    def _():
        for cp in kept_copies():
            cp.wait()


def join_kernel(r0, count, lt, nblk, na, *refs):
    blocks, (whole, final, loads) = refs[:7], refs[7:10]
    result, gores = refs[10:12]
    scratch = refs[12:28]
    row_out, stage, stage_near, row_sem, come, go, come_near, go_near = refs[28:]
    share = stage_near.shape[3]
    i = pl.program_id(0)

    def in_copies():
        return [pltpu.make_async_copy(whole.at[:, r], stage.at[r - NF], come.at[r - NF])
                for r in range(NF, r0)] + [
            pltpu.make_async_copy(final.at[g], stage_near.at[g], come_near.at[g]) for g in range(na)]

    def out_copies():
        return [pltpu.make_async_copy(stage.at[r - NF], result.at[:, r], go.at[r - NF])
                for r in range(NF, r0)] + [
            pltpu.make_async_copy(
                stage_near.at[g], result.at[:, pl.ds(0, NF), pl.ds(g * share, share), :], go_near.at[g])
            for g in range(na)]

    def row_copy(j):
        return pltpu.make_async_copy(row_out.at[j], result.at[:, r0 + j], row_sem.at[j])

    @pl.when(i == 0)
    def _():
        gores[...] = loads[0:1, 0:GORES].reshape(GORES)
        for cp in in_copies():
            cp.start()

    @pl.when(i == 1)
    def _():
        for cp in in_copies():
            cp.wait()
        for cp in out_copies():
            cp.start()

    row_step(i, r0, count, lt, nblk, blocks, row_out.at[i], scratch)
    row_copy(i).start()

    @pl.when(i == count - 1)
    def _():
        for cp in out_copies():
            cp.wait()
        for j in range(count):
            row_copy(j).wait()


def row_call(kernel, name, r0, count, args, extra, extra_specs, out_shape, out_specs, more, **params):
    state = args[0]
    _, rows, stations, cells = state.shape
    lt = cells // 128
    nblk = stations // SB
    f32 = jnp.float32
    row_spec = pl.BlockSpec((5, None, stations, cells), lambda i: (0, r0 + i, 0, 0))
    ahead_spec = pl.BlockSpec((5, None, stations, cells), lambda i: (0, r0 + (i + 1) % count, 0, 0))
    end_spec = pl.BlockSpec((5, None, SB, cells), lambda i: (0, r0 + i, 0, 0))
    pack_spec = pl.BlockSpec((nblk // 2, 5, 2 * SB, 128), lambda i: (0, 0, 0, 0))
    field = pltpu.VMEM((lt, stations + 2 * SB, 128), f32)
    group = pltpu.VMEM((5, lt, stations + 2 * SB, 128), f32)
    field_z = pltpu.VMEM((1, cells + 2 * SB, stations), f32)
    group_z = pltpu.VMEM((5, 1, cells + 2 * SB, stations), f32)
    return pl.pallas_call(
        kernel,
        out_shape=out_shape,
        grid=(count,),
        in_specs=[row_spec, ahead_spec, end_spec, end_spec, pack_spec, pack_spec, row_spec] + extra_specs,
        out_specs=out_specs(row_spec),
        scratch_shapes=[group] * 5 + [field] + [group_z] * 5 + [
            field_z,
            pltpu.VMEM((5, cells, stations), f32),
            pltpu.VMEM((5, lt, stations, 128), f32),
            pltpu.VMEM((5, 128, stations), f32),
            pltpu.VMEM((5, 128, stations), f32),
        ] + more,
        compiler_params=pltpu.CompilerParams(
            dimension_semantics=("arbitrary",), vmem_limit_bytes=63 << 20, **params),
        name=name,
    )(state, *args, *extra)


def rk_rows(state, lo, hi, left, right, part, cutoff, near_rows, loads, na):
    _, rows, stations, cells = state.shape
    lt = cells // 128
    nblk = stations // SB
    share = stations // na
    f32 = jnp.float32
    count = rows - 2
    middle = NF + 2 * (count - NF) // 5
    args = [state, lo, hi, left, right, part]
    any_spec = pl.BlockSpec(memory_space=pl.ANY)
    shape = (na, 5, NF, share, cells)
    pieces = pltpu.VMEM(shape, f32)
    whole_shape = jax.ShapeDtypeStruct(state.shape, f32)
    dma = pltpu.SemaphoreType.DMA
    whole, final = row_call(
        functools.partial(send_kernel, count, middle, lt, nblk, na), "rows_send", 0, count, args,
        [cutoff, near_rows[None], *(jnp.asarray(t) for t in mode_tables())],
        [pl.BlockSpec(cutoff.shape, lambda i: (0, 0)), pl.BlockSpec((1, stations), lambda i: (0, 0))]
        + [any_spec] * 4,
        (whole_shape, jax.ShapeDtypeStruct(shape, f32)),
        lambda row_spec: (row_spec, any_spec),
        [
            pltpu.VMEM((NF, 5, stations, cells), f32),
            pieces, pieces,
            pltpu.VMEM((2, 5 * NF * share, NA // 4), f32),
            pltpu.VMEM((4, NA // 2, NA // 4), jnp.bfloat16),
            pltpu.VMEM((stations, 2 * NF), f32),
            dma((na - 1, NF)), dma((na - 1, NF)), dma((NF + 1,)),
            dma((na - 1,)), dma((na - 1,)), dma((4,)),
        ],
        collective_id=1, has_side_effects=True)
    return row_call(
        functools.partial(join_kernel, count, rows - count, lt, nblk, na), "rows_join",
        count, rows - count, args,
        [whole, final, loads],
        [any_spec, any_spec, pl.BlockSpec((SB, 128), lambda i: (0, 0))],
        (whole_shape, jax.ShapeDtypeStruct((GORES,), f32)),
        lambda row_spec: (any_spec, pl.BlockSpec((GORES,), lambda i: (0,))),
        [
            pltpu.VMEM((rows - count, 5, stations, cells), f32),
            pltpu.VMEM((count - NF, 5, stations, cells), f32),
            pieces,
            dma((rows - count,)), dma((count - NF,)), dma((count - NF,)), dma((na,)), dma((na,)),
        ])


def mode_tables():
    n = np.arange(NA // 2)[:, None]
    tables = []
    for parity in (0, 1):
        k = np.arange(parity, NA // 4, 2)[None, :]
        angle = 2.0 * math.pi / NA * ((n * k) % NA)
        table = np.concatenate([np.cos(angle), np.sin(angle)], axis=1).astype(np.float32)
        high = table.astype(jnp.bfloat16)
        tables += [high, (table - high.astype(np.float32)).astype(jnp.bfloat16)]
    return tables


def split(x):
    high = x.astype(jnp.bfloat16)
    return high, (x - high.astype(jnp.float32)).astype(jnp.bfloat16)


def product(x, y, dims):
    x_high, x_low = x
    y_high, y_low = y

    def dot(a, b):
        return lax.dot_general(a, b, (dims, ((), ())), preferred_element_type=jnp.float32)

    return dot(x_high, y_high) + (dot(x_low, y_high) + dot(x_high, y_low))


def low_pass(x, out, coef, tables, turned, cutoff, near_rows):
    pieces, _, _, share, cells = x.shape
    m = 5 * NF * share
    half = pieces // 2
    modes = tables.shape[2] // 2
    chosen = lax.broadcasted_iota(jnp.int32, cutoff.shape, 0) < near_rows[...]
    signed = jnp.where(chosen, cutoff[...], -cutoff[...]).astype(jnp.float32)
    turned[...] = jnp.concatenate([signed, signed], axis=0).T
    here = turned[pl.ds(pl.multiple_of(lax.axis_index("az") * share, SB), share), :]
    signs = jnp.concatenate([here[:, j:j + 1] for j in range(NF)] * 5, axis=0)
    limit = jnp.abs(signs).astype(jnp.int32)
    take = signs > 0.0

    for p in range(half):
        x0 = x[p].reshape(m, cells)
        x1 = x[p + half].reshape(m, cells)
        at = slice(p * cells, (p + 1) * cells)
        for parity, part in enumerate((x0 + x1, x0 - x1)):
            rhs = (tables[2 * parity, at, :], tables[2 * parity + 1, at, :])
            value = product(split(part), rhs, ((1,), (0,)))
            coef[parity] = value if p == 0 else coef[parity] + value
    column = lax.broadcasted_iota(jnp.int32, (m, 2 * modes), 1)
    column = jnp.where(column < modes, column, column - modes)
    back = []
    for parity in range(2):
        k = 2 * column + parity
        weight = jnp.where(k == 0, 1.0 / NA, 2.0 / NA)
        gains = jnp.where(k < limit, weight, 0.0)
        back.append(split(coef[parity] * gains))
    for p in range(half):
        at = slice(p * cells, (p + 1) * cells)
        y0, y1 = (
            product(back[parity], (tables[2 * parity, at, :], tables[2 * parity + 1, at, :]), ((1,), (1,)))
            for parity in range(2)
        )
        for q, y in ((p, y0 + y1), (p + half, y0 - y1)):
            kept = jnp.where(take, y, x[q].reshape(m, cells))
            out[q] = kept.reshape(5, NF, share, cells)


def pressure_of(conserved):
    density = conserved[0]
    kinetic = (
        0.5
        * (conserved[1] * conserved[1] + conserved[2] * conserved[2] + conserved[3] * conserved[3])
        / density
    )
    return (HEAT_RATIO - 1.0) * (conserved[4] - kinetic)


def per_device(step_start, section_state, near_rows, cutoff, gore_map):
    _, rows, stations, cells = section_state.shape
    na, nx = lax.axis_size("az"), lax.axis_size("ax")
    line_index = lax.axis_index("ax")
    canopy = rows // 2
    jump = pressure_of(section_state[:, canopy - 1]) - pressure_of(section_state[:, canopy + 1])
    total = stations * nx
    station = line_index * stations + jnp.arange(stations, dtype=jnp.int32)
    ramp = 1.0 + 2.0 * station.astype(jnp.float32) / total
    weighted = jump * ramp[:, None] * (1.0 / math.sqrt(total * NA / GORES))
    gores = jnp.arange(GORES, dtype=jnp.int32)
    partial = jnp.sum(
        jnp.where(gore_map[None] == gores[:, None, None], weighted[None], 0.0), axis=(1, 2))
    part, left, right, lo, hi, loads = radial_part(section_state, step_start, partial, na, nx)

    return tuple(rk_rows(
        section_state, lo, hi, left, right, part, cutoff, near_rows, loads, na))


def solution(mesh):
    in_specs = (
        P(None, None, "ax", "az"),
        P(None, None, "ax", "az"),
        P("ax"),
        P(None, "ax"),
        P("ax", "az"),
    )
    out_specs = (P(None, None, "ax", "az"), P())
    return jax.shard_map(
        per_device, mesh=mesh, in_specs=in_specs, out_specs=out_specs, check_vma=False
    )
```
